32 devices in a mesh: sec: 8 (over z, y), tile: 4 (over x, core).
Axes of the slice: x: 2, y: 2, z: 4, core: 2. Of those that a mesh axis runs over, the one named last changes fastest.
Arguments:
- image: bfloat16 [8, 1024, 1024], P('sec', 'tile'), may hold values from -6 to 6
- weight: bfloat16 [8, 1024, 1024], P('sec', 'tile'), may hold values from 0.25 to 4
- lens_filter_taps: float32 [8, 4, 25], P('sec', 'tile'), may hold values from -2 to 2
- block_src: int32 [8, 4, 4, 2], P('sec', 'tile'), may hold values from 0 to 15
- block_dst: int32 [8, 4, 4, 2], P('sec', None, 'tile'), may hold values from 0 to 3, as said below
- valid_count: int32 [8, 4, 4], P('sec', 'tile'), may hold values from 1 to 2, as said below
- anchor: bfloat16 [16, 128, 128], P('tile'), may hold values from -6 to 6
Outputs:
- correlation: float32 [8, 32, 128, 128], P('sec', 'tile')
The draws below stay inside these ranges and needn't reach their ends.
Inputs may be any that keep to these rules, and one draw needn't show every extreme that they name: `block_dst`: every block of every strip receives at least one live slot. `valid_count`: in every section some strip receives 2 live slots from every tile; block_src and block_dst are 0 in slots at or beyond the valid count.
All inputs are finite; a program needn't handle non-finite values.
Results may differ from the reference program's by a relative error of at most 0.02.
Values may be sent and summed in bfloat16 or wider, within the bound.
A program may use at most 64 MiB of HBM per device.

```python
import math
import jax
import jax.numpy as jnp
from jax import lax

B = 128
CAP = 2
TH = 256
TW = 1024
TB = 16
SB = 4
SECTION_COUNT = 8
TILES = 4
ROWS = 1024


def placement_lists(key):
    pieces = jax.random.split(jax.random.fold_in(key, 7), 5)
    counts = jax.random.randint(pieces[0], (SECTION_COUNT, TILES, TILES), 1, CAP + 1)
    hot_strip = jax.random.randint(pieces[1], (SECTION_COUNT,), 0, TILES)
    is_hot = jnp.arange(TILES)[None, None, :] == hot_strip[:, None, None]
    counts = jnp.where(is_hot, CAP, counts).astype(jnp.int32)
    source_ids = jax.random.randint(pieces[2], (SECTION_COUNT, TILES, TILES, CAP), 0, TB)
    dest_ids = jax.random.randint(pieces[3], (SECTION_COUNT, TILES, TILES, CAP), 0, SB)
    offsets = jax.random.randint(pieces[4], (SECTION_COUNT,), 0, SB)
    tile_index = jnp.arange(TILES, dtype=jnp.int32)
    first_dest = (tile_index[None, :, None] + tile_index[None, None, :] + offsets[:, None, None]) % SB
    is_first = jnp.arange(CAP)[None, None, None, :] == 0
    dest_ids = jnp.where(is_first, first_dest[..., None], dest_ids)
    is_live = jnp.arange(CAP)[None, None, None, :] < counts[..., None]
    source_ids = jnp.where(is_live, source_ids, 0).astype(jnp.int32)
    dest_ids = jnp.where(is_live, dest_ids, 0).astype(jnp.int32)
    return (source_ids, dest_ids, counts)


def draw_block_src(key, part):
    return placement_lists(key)[0]


def draw_block_dst(key, part):
    return placement_lists(key)[1]


def draw_valid_count(key, part):
    return placement_lists(key)[2]


def steps_of(rng, dims, cuts, smallest, largest):
    def one(axis_at, blocks):
        draws = jax.random.uniform(jax.random.fold_in(jax.random.fold_in(rng, 6), axis_at), (blocks,), jnp.float32, smallest / len(cuts), largest / len(cuts))
        return jnp.repeat(jnp.exp(draws), dims[axis_at] // blocks).reshape((-1,) + (1,) * (len(dims) - axis_at - 1))

    factor_of = one(*cuts[0])
    for cut in cuts[1:]:
        factor_of = factor_of * one(*cut)
    return factor_of


def normal_values(stream_key, dims, width, most, cuts=(), kind=jnp.bfloat16):
    values = width * jax.random.normal(stream_key, dims, jnp.float32)
    if cuts:
        values = values * steps_of(stream_key, dims, cuts, -0.22, 0.18)
    return jnp.clip(values, -most, most).astype(kind)


def setup_inputs(seed: int = 0) -> dict:
    key_list = jax.random.split(jax.random.key(seed), 8)
    return {
        "image": normal_values(key_list[0], (SECTION_COUNT, ROWS, TW), 1.0, 6.0, ((0, 8), (1, 4))),
        "weight": jnp.clip(jnp.exp(math.log(4.0) - 2.7725887 * jax.random.uniform(key_list[1], (SECTION_COUNT, ROWS, TW), jnp.float32) ** steps_of(key_list[1], (SECTION_COUNT, ROWS, TW), ((0, 8), (1, 4)), -0.2, 0.2)), 0.25, 4.0).astype(jnp.bfloat16),
        "lens_filter_taps": normal_values(key_list[2], (SECTION_COUNT, TILES, 25), 0.4, 2.0, ((0, 8), (1, 4)), jnp.float32),
        "block_src": draw_block_src(jax.random.fold_in(key_list[7], 71), 0),
        "block_dst": draw_block_dst(jax.random.fold_in(key_list[7], 71), 0),
        "valid_count": draw_valid_count(jax.random.fold_in(key_list[7], 71), 0),
        "anchor": normal_values(key_list[6], (TILES * SB, B, B), 1.0, 6.0, ((0, 4),)),
    }


def render_section(operands):
    section_image, section_weight, kernel_taps, source_ids, dest_ids, counts = operands
    rows_total = section_image.shape[0]
    padded = jnp.pad(section_image, 2)
    row_taps = jnp.repeat(kernel_taps, TH, axis=0)
    corrected = jnp.zeros((rows_total, TW), jnp.float32)
    for row_off in range(5):
        for col_off in range(5):
            corrected = corrected + row_taps[:, row_off * 5 + col_off][:, None] * padded[row_off:row_off + rows_total, col_off:col_off + TW].astype(jnp.float32)
    weighted = (corrected * section_weight.astype(jnp.float32)).astype(jnp.bfloat16)
    tile_blocks = weighted.reshape(TILES, TH // B, B, TW // B, B).transpose(0, 1, 3, 2, 4).reshape(TILES, TB, B, B)
    picked = tile_blocks[jnp.arange(TILES)[:, None, None], source_ids]
    is_live = jnp.arange(CAP)[None, None, :] < counts[:, :, None]
    picked = jnp.where(is_live[..., None, None], picked, jnp.zeros_like(picked))
    indicator_vector = ((dest_ids[..., None] == jnp.arange(SB)[None, None, None, :]) & is_live[..., None]).astype(jnp.float32)
    strips = jnp.einsum('tdcs,tdcxy->dsxy', indicator_vector, picked.astype(jnp.float32))
    return strips.reshape(TILES * SB, B, B).astype(jnp.bfloat16)

def window_set(strips):
    extended = jnp.concatenate([strips, jnp.zeros_like(strips[:1])], 0)
    aligned = extended[:-1]
    half_shift = jnp.concatenate([extended[:-1, :, B // 2:], extended[1:, :, :B // 2]], 2)
    return jnp.stack([aligned, half_shift], 1).reshape(-1, B, B)

def exact_table(table):
    high = table.astype(jnp.bfloat16)
    low = (table - high.astype(jnp.float32)).astype(jnp.bfloat16)
    return high.astype(jnp.float32) + low.astype(jnp.float32)

def base_tables():
    positions = jnp.arange(B, dtype=jnp.int32)
    product = positions[:, None] * positions[None, :] % B
    angle = product.astype(jnp.float32) * (2.0 * math.pi / B)
    return (jnp.cos(angle), jnp.sin(angle))

def to_half(values):
    return lax.optimization_barrier(values.astype(jnp.bfloat16)).astype(jnp.float32)

def right_mult(data, table):
    return jnp.einsum('wjk,kl->wjl', data, table, precision=lax.Precision.HIGHEST)

def left_mult(table, data):
    return jnp.einsum('jk,wkl->wjl', table, data, precision=lax.Precision.HIGHEST)

def forward(windows):
    cosine, sine_table = base_tables()
    pair_right = exact_table(jnp.concatenate([cosine, sine_table], 1))
    pair_left = exact_table(jnp.concatenate([cosine, sine_table], 0))
    right = to_half(right_mult(windows.astype(jnp.float32), pair_right))
    from_cos = left_mult(pair_left, right[:, :, :B])
    from_sin = left_mult(pair_left, right[:, :, B:])
    spec_re = from_cos[:, :B] - from_sin[:, B:]
    spec_im = -(from_cos[:, B:] + from_sin[:, :B])
    return (spec_re, spec_im)

def correlate(operands):
    current, earlier = operands
    cur_re, cur_im = forward(window_set(current))
    pre_re, pre_im = forward(window_set(earlier))
    cross_re = cur_re * pre_re + cur_im * pre_im
    cross_im = cur_im * pre_re - cur_re * pre_im
    magnitude = jnp.sqrt(cross_re * cross_re + cross_im * cross_im)
    mean_mag = lax.optimization_barrier(jnp.mean(magnitude, axis=(1, 2), keepdims=True))
    denominator = magnitude + 0.1 * mean_mag + 1e-06
    whitened = to_half(jnp.concatenate([cross_re / denominator, cross_im / denominator], 2))
    cosine, sine_table = base_tables()
    inverse_right = exact_table(jnp.concatenate([jnp.concatenate([cosine, sine_table], 1), jnp.concatenate([-sine_table, cosine], 1)], 0))
    inverse_left = exact_table(jnp.concatenate([cosine, -sine_table], 1))
    rows_both = to_half(right_mult(whitened, inverse_right))
    stacked = jnp.concatenate([rows_both[:, :, :B], rows_both[:, :, B:]], 1)
    return (left_mult(inverse_left, stacked) / B).astype(jnp.float32)

def reference(image, weight, lens_filter_taps, block_src, block_dst, valid_count, anchor):
    gathered_strip_list = lax.map(render_section, (image, weight, lens_filter_taps, block_src, block_dst, valid_count))
    earlier = jnp.concatenate([anchor[None], gathered_strip_list[:-1]], 0)
    return lax.map(correlate, (gathered_strip_list, earlier))
```

```python
import functools
import math

import jax
import jax.numpy as jnp
import numpy as np
from jax import lax
from jax.experimental import pallas as pl
from jax.experimental.pallas import tpu as pltpu
from jax.sharding import PartitionSpec as P

MESH = pl.DeviceIdType.MESH
EDGE = 16
LANES = 128


def repeat(count, step):
    if count <= 4:
        for i in range(count):
            step(i)
    else:
        pl.loop(0, count)(step)


def dft_tables(size):
    positions = np.arange(size)
    angle = (positions[:, None] * positions[None, :] % size) * (2.0 * math.pi / size)
    cosine, sine = np.cos(angle), np.sin(angle)
    inverse_right = np.block([[cosine, sine], [-sine, cosine]])
    forward_left = np.block([[cosine, -sine], [-sine, -cosine]])
    return jnp.asarray(np.concatenate([inverse_right, forward_left], 0), jnp.bfloat16)


def lens(rows, taps, first, count):
    left, middle, right = rows
    lane = lax.broadcasted_iota(jnp.int32, middle.shape, 1)
    shifted = []
    for off in range(-2, 3):
        if off == 0:
            shifted.append(middle)
        elif off > 0:
            mixed = jnp.where(lane < off, right, middle)
            shifted.append(pltpu.roll(mixed, LANES - off, 1))
        else:
            mixed = jnp.where(lane >= LANES + off, left, middle)
            shifted.append(pltpu.roll(mixed, -off, 1))
    total = None
    n = middle.shape[0]
    for a in range(5):
        part = taps[5 * a] * shifted[0]
        for b in range(1, 5):
            part = part + taps[5 * a + b] * shifted[b]
        if a != 2:
            part = pltpu.roll(part, (2 - a) % n, 0)
        part = part[first : first + count]
        total = part if total is None else total + part
    return total


def kernel(
    sections,
    tiles,
    image,
    weight,
    anchor,
    tables,
    taps_ref,
    src_ref,
    dst_ref,
    valid_ref,
    out,
    img,
    wgt,
    halo,
    out_mid,
    out_edge,
    in_mid,
    in_edge,
    strip,
    pre,
    spec,
    tab,
    load_sem,
    halo_send,
    halo_recv,
    mid_send,
    mid_recv,
    edge_send,
    edge_recv,
    strip_send,
    strip_recv,
):
    sec = lax.axis_index("sec")
    me = lax.axis_index("tile")
    th, tw = image.shape[1:]
    side = strip.shape[1]
    blocks = strip.shape[0] - 1
    cap = in_mid.shape[1]
    across, down = tw // side, th // side
    padded = across + 2
    mid = side - 2 * EDGE

    barrier = pltpu.get_barrier_semaphore()

    def greet(target):
        pl.semaphore_signal(barrier, inc=1, device_id=target, device_id_type=MESH)

    for k in range(1, tiles):
        greet((sec, lax.rem(me + k, tiles)))
    has_next, has_prev = sec < sections - 1, sec > 0
    not_first, not_last = me > 0, me < tiles - 1

    @pl.when(has_next)
    def _():
        greet((sec + 1, me))

    @pl.when(has_next & not_first)
    def _():
        greet((sec + 1, me - 1))

    @pl.when(has_prev)
    def _():
        greet((sec - 1, me))

    @pl.when(has_prev & not_last)
    def _():
        greet((sec - 1, me + 1))

    loads = []
    for r in range(down):
        low, high = max(0, r * side - EDGE), min(th, (r + 1) * side + EDGE)
        place = low - (r * side - EDGE)
        for c in range(across):
            columns = pl.ds(c * side, side)
            loads.append(
                pltpu.make_async_copy(
                    image.at[0, pl.ds(low, high - low), columns],
                    img.at[r * padded + c + 1, pl.ds(place, high - low)],
                    load_sem.at[len(loads)],
                )
            )
            loads.append(
                pltpu.make_async_copy(
                    weight.at[0, pl.ds(r * side, side), columns],
                    wgt.at[r * across + c],
                    load_sem.at[len(loads)],
                )
            )
    table_load = pltpu.make_async_copy(tables, tab, load_sem.at[len(loads)])
    for load in loads:
        load.start()
    table_load.start()

    anchor_load = pltpu.make_async_copy(anchor, pre.at[pl.ds(0, blocks)], strip_recv.at[1])

    @pl.when(sec == 0)
    def _():
        anchor_load.start()

    zeros = jnp.zeros(img.shape[1:], img.dtype)
    for r in range(down):
        img[r * padded] = zeros
        img[(r + 1) * padded - 1] = zeros

    @pl.when(me == 0)
    def _():
        for c in range(across):
            img[c + 1, :EDGE] = zeros[:EDGE]

    @pl.when(me == tiles - 1)
    def _():
        for c in range(across):
            img[(down - 1) * padded + c + 1, EDGE + side :] = zeros[:EDGE]
        strip[blocks] = jnp.zeros((side, side), strip.dtype)
        pre[blocks] = jnp.zeros((side, side), pre.dtype)

    after, before = has_next.astype(jnp.int32), has_prev.astype(jnp.int32)
    peers = after * (1 + not_first.astype(jnp.int32)) + before * (1 + not_last.astype(jnp.int32))
    pl.semaphore_wait(barrier, tiles - 1 + peers)

    def remote(src, dst, send, recv, target):
        return pltpu.make_async_remote_copy(
            src_ref=src,
            dst_ref=dst,
            send_sem=send,
            recv_sem=recv,
            device_id=target,
            device_id_type=MESH,
        )

    halo_down = remote(
        image.at[0, pl.ds(th - EDGE, EDGE)],
        halo.at[0],
        halo_send.at[0],
        halo_recv.at[0],
        (sec, lax.rem(me + 1, tiles)),
    )
    halo_up = remote(
        image.at[0, pl.ds(0, EDGE)],
        halo.at[1],
        halo_send.at[1],
        halo_recv.at[1],
        (sec, lax.rem(me + tiles - 1, tiles)),
    )
    anchor_rim = remote(
        anchor.at[0],
        pre.at[blocks],
        strip_send.at[2],
        strip_recv.at[2],
        (sec, lax.rem(me + tiles - 1, tiles)),
    )

    @pl.when(not_last)
    def _():
        halo_down.start()

    @pl.when(not_first)
    def _():
        halo_up.start()

    @pl.when((sec == 0) & not_first)
    def _():
        anchor_rim.start()

    for load in loads:
        load.wait()

    taps = [taps_ref[0, 0, k] for k in range(25)]
    chips = tiles // 2

    def owner(k):
        chip = lax.rem(me // 2 + 1 + k // 2, chips)
        return chip * 2 + lax.rem(me + 1 + k, 2)

    def picked(target, slot, first, count):
        source = src_ref[0, 0, target, slot]
        place = source + 2 * lax.div(source, across)
        rows = [
            img[place + k, first : first + count + 2 * EDGE].astype(jnp.float32) for k in range(3)
        ]
        rows = [part[EDGE - 8 : EDGE + count + 8] for part in rows]
        corrected = lens(rows, taps, 8, count)
        factor = wgt[source, first : first + count].astype(jnp.float32)
        live = jnp.clip(valid_ref[0, 0, target] - slot, 0, 1).astype(jnp.float32)
        return (corrected * factor * live).astype(jnp.bfloat16)

    def mid_copy(k):
        target = owner(k)
        return remote(
            out_mid.at[target], in_mid.at[me], mid_send.at[target], mid_recv.at[me], (sec, target)
        )

    def edge_copy(k):
        target = owner(k)
        return remote(
            out_edge.at[target],
            in_edge.at[me],
            edge_send.at[target],
            edge_recv.at[me],
            (sec, target),
        )

    def fill_mid(k, ref, place):
        for slot in range(cap):
            for piece in range(0, mid, 32):
                ref[place, slot, piece : piece + 32] = picked(owner(k), slot, EDGE + piece, 32)

    def fill_edge(k, ref, place):
        for slot in range(cap):
            ref[place, slot, :EDGE] = picked(owner(k), slot, 0, EDGE)
            ref[place, slot, EDGE:] = picked(owner(k), slot, side - EDGE, EDGE)

    def send_mid(k):
        fill_mid(k, out_mid, owner(k))
        mid_copy(k).start()

    pl.loop(0, tiles - 1)(send_mid)

    @pl.when(not_first)
    def _():
        halo_down.wait_recv()
        for c in range(across):
            img[c + 1, :EDGE] = halo[0, :, c * side : (c + 1) * side]

    @pl.when(not_last)
    def _():
        halo_up.wait_recv()
        for c in range(across):
            img[(down - 1) * padded + c + 1, EDGE + side :] = halo[
                1, :, c * side : (c + 1) * side
            ]

    def send_edge(k):
        fill_edge(k, out_edge, owner(k))
        edge_copy(k).start()

    pl.loop(0, tiles - 1)(send_edge)
    fill_mid(tiles - 1, in_mid, me)
    fill_edge(tiles - 1, in_edge, me)

    def summed(ref, start, count):
        totals = [None] * blocks
        for t in range(tiles):
            for slot in range(cap):
                value = ref[t, slot, pl.ds(start, count)].astype(jnp.float32)
                place = dst_ref[0, t, 0, slot]
                for j in range(blocks):
                    term = value * (1 - jnp.minimum(jnp.abs(place - j), 1)).astype(jnp.float32)
                    totals[j] = term if totals[j] is None else totals[j] + term
        return [total.astype(strip.dtype) for total in totals]

    def arrive(copy_of):
        def step(k):
            source = owner(k)
            copy_of(k, source).wait_recv()

        return step

    def mid_from(k, source):
        return remote(
            out_mid.at[source], in_mid.at[source], mid_send.at[source], mid_recv.at[source], (sec, source)
        )

    def edge_from(k, source):
        return remote(
            out_edge.at[source], in_edge.at[source], edge_send.at[source], edge_recv.at[source], (sec, source)
        )

    repeat(tiles - 1, arrive(mid_from))
    for piece in range(0, mid, 32):
        for j, value in enumerate(summed(in_mid, piece, 32)):
            strip[j, EDGE + piece : EDGE + piece + 32] = value
    repeat(tiles - 1, arrive(edge_from))
    for j, value in enumerate(summed(in_edge, 0, 2 * EDGE)):
        strip[j, :EDGE] = value[:EDGE]
        strip[j, side - EDGE :] = value[EDGE:]

    onward = remote(
        strip.at[pl.ds(0, blocks)],
        pre.at[pl.ds(0, blocks)],
        strip_send.at[1],
        strip_recv.at[1],
        (lax.rem(sec + 1, sections), me),
    )
    rim = remote(
        strip.at[0],
        strip.at[blocks],
        strip_send.at[0],
        strip_recv.at[0],
        (sec, lax.rem(me + tiles - 1, tiles)),
    )
    onward_rim = remote(
        strip.at[0],
        pre.at[blocks],
        strip_send.at[3],
        strip_recv.at[2],
        (lax.rem(sec + 1, sections), lax.rem(me + tiles - 1, tiles)),
    )

    @pl.when(not_first)
    def _():
        rim.start()

    @pl.when(has_next & not_first)
    def _():
        onward_rim.start()

    @pl.when(has_next)
    def _():
        onward.start()

    table_load.wait()
    right_table = tab.at[pl.ds(0, 2 * side)]
    left_table = tab.at[pl.ds(2 * side, 2 * side)]

    def spectra(ref, m):
        block, after = ref[m], ref[m + 1]
        lane = lax.broadcasted_iota(jnp.int32, block.shape, 1)
        shifted = jnp.where(
            lane < side // 2, after.astype(jnp.float32), block.astype(jnp.float32)
        ).astype(block.dtype)
        windows = jnp.concatenate([block, shifted], 0)
        right = jnp.dot(
            windows, right_table[:side], preferred_element_type=jnp.float32
        ).astype(jnp.bfloat16)
        stacked = jnp.concatenate(
            [
                jnp.concatenate([right[:side, :side], right[:side, side:]], 0),
                jnp.concatenate([right[side:, :side], right[side:, side:]], 0),
            ],
            1,
        )
        return jnp.dot(left_table[...], stacked, preferred_element_type=jnp.float32)

    def keep(m):
        spec[m] = spectra(strip, m)

    repeat(blocks - 1, keep)

    @pl.when(not_last)
    def _():
        rim.wait_recv()

    keep(blocks - 1)

    @pl.when(has_prev)
    def _():
        onward.wait_recv()

    @pl.when(sec == 0)
    def _():
        anchor_load.wait()

    @pl.when(not_last)
    def _():
        anchor_rim.wait_recv()

    def correlate(m):
        earlier = spectra(pre, m)
        current = spec[m]
        cur_re, cur_im = current[:side], current[side:]
        pre_re, pre_im = earlier[:side], earlier[side:]
        cross_re = cur_re * pre_re + cur_im * pre_im
        cross_im = cur_im * pre_re - cur_re * pre_im
        magnitude = jnp.sqrt(cross_re * cross_re + cross_im * cross_im)
        whitened = []
        for half in range(2):
            cols = slice(half * side, (half + 1) * side)
            mag = magnitude[:, cols]
            mean = jnp.sum(mag) * (1.0 / (side * side))
            scale = (1.0 / side) / (mag + (0.1 * mean + 1e-06))
            whitened.append(
                jnp.concatenate([cross_re[:, cols] * scale, cross_im[:, cols] * scale], 1)
            )
        whitened = jnp.concatenate(whitened, 0).astype(jnp.bfloat16)
        rows = jnp.dot(
            whitened, right_table[...], preferred_element_type=jnp.float32
        ).astype(jnp.bfloat16)
        stacked = jnp.concatenate(
            [
                jnp.concatenate([rows[:side, :side], rows[:side, side:]], 0),
                jnp.concatenate([rows[side:, :side], rows[side:, side:]], 0),
            ],
            1,
        )
        result = jnp.dot(left_table[:side], stacked, preferred_element_type=jnp.float32)
        out[0, 2 * m] = result[:, :side]
        out[0, 2 * m + 1] = result[:, side:]

    repeat(blocks, correlate)

    @pl.when(not_last)
    def _():
        halo_down.wait_send()

    @pl.when(not_first)
    def _():
        halo_up.wait_send()
        rim.wait_send()

    @pl.when((sec == 0) & not_first)
    def _():
        anchor_rim.wait_send()

    @pl.when(has_next)
    def _():
        onward.wait_send()

    @pl.when(has_next & not_first)
    def _():
        onward_rim.wait_send()

    def left_here(k):
        mid_copy(k).wait_send()
        edge_copy(k).wait_send()

    repeat(tiles - 1, left_here)


def solution(mesh):
    sections, tiles = mesh.shape["sec"], mesh.shape["tile"]

    def body(image, weight, lens_filter_taps, block_src, block_dst, valid_count, anchor):
        th, tw = image.shape[1:]
        blocks, side = anchor.shape[:2]
        cap = block_src.shape[-1]
        anywhere = pl.BlockSpec(memory_space=pl.ANY)
        scalars = pl.BlockSpec(memory_space=pltpu.SMEM)
        bf16 = jnp.bfloat16
        dma = pltpu.SemaphoreType.DMA
        mid = side - 2 * EDGE
        across, down = tw // side, th // side
        return pl.pallas_call(
            functools.partial(kernel, sections, tiles),
            out_shape=jax.ShapeDtypeStruct((1, 2 * blocks, side, side), jnp.float32),
            in_specs=[anywhere] * 4 + [scalars] * 4,
            out_specs=pl.BlockSpec(memory_space=pltpu.VMEM),
            scratch_shapes=[
                pltpu.VMEM((down * (across + 2), side + 2 * EDGE, side), bf16),
                pltpu.VMEM((down * across, side, side), bf16),
                pltpu.VMEM((2, EDGE, tw), bf16),
                pltpu.VMEM((tiles, cap, mid, side), bf16),
                pltpu.VMEM((tiles, cap, 2 * EDGE, side), bf16),
                pltpu.VMEM((tiles, cap, mid, side), bf16),
                pltpu.VMEM((tiles, cap, 2 * EDGE, side), bf16),
                pltpu.VMEM((blocks + 1, side, side), bf16),
                pltpu.VMEM((blocks + 1, side, side), bf16),
                pltpu.VMEM((blocks, 2 * side, 2 * side), jnp.float32),
                pltpu.VMEM((4 * side, 2 * side), bf16),
                dma((2 * down * across + 1,)),
                dma((2,)),
                dma((2,)),
                dma((tiles,)),
                dma((tiles,)),
                dma((tiles,)),
                dma((tiles,)),
                dma((4,)),
                dma((3,)),
            ],
            compiler_params=pltpu.CompilerParams(collective_id=0, has_side_effects=True),
        )(
            image,
            weight,
            anchor,
            dft_tables(side),
            lens_filter_taps,
            block_src,
            block_dst,
            valid_count,
        )

    in_specs = (
        P("sec", "tile", None),
        P("sec", "tile", None),
        P("sec", "tile", None),
        P("sec", "tile", None, None),
        P("sec", None, "tile", None),
        P("sec", "tile", None),
        P("tile", None, None),
    )
    out_specs = P("sec", "tile", None, None)
    return jax.shard_map(body, mesh=mesh, in_specs=in_specs, out_specs=out_specs, check_vma=False)
```

```python
import functools
import math

import jax
import jax.numpy as jnp
import numpy as np
from jax import lax
from jax.experimental import pallas as pl
from jax.experimental.pallas import tpu as pltpu
from jax.sharding import PartitionSpec as P

MESH = pl.DeviceIdType.MESH
EDGE = 16
LANES = 128


def repeat(count, step):
    if count <= 4:
        for i in range(count):
            step(i)
    else:
        pl.loop(0, count)(step)


def dft_tables(size):
    positions = np.arange(size)
    angle = (positions[:, None] * positions[None, :] % size) * (2.0 * math.pi / size)
    cosine, sine = np.cos(angle), np.sin(angle)
    inverse_right = np.block([[cosine, sine], [-sine, cosine]])
    forward_left = np.block([[cosine, -sine], [-sine, -cosine]])
    return jnp.asarray(np.concatenate([inverse_right, forward_left], 0), jnp.bfloat16)


def lens(rows, taps, first, count):
    left, middle, right = rows
    lane = lax.broadcasted_iota(jnp.int32, middle.shape, 1)
    shifted = []
    for off in range(-2, 3):
        if off == 0:
            shifted.append(middle)
        elif off > 0:
            mixed = jnp.where(lane < off, right, middle)
            shifted.append(pltpu.roll(mixed, LANES - off, 1))
        else:
            mixed = jnp.where(lane >= LANES + off, left, middle)
            shifted.append(pltpu.roll(mixed, -off, 1))
    total = None
    n = middle.shape[0]
    for a in range(5):
        part = taps[5 * a] * shifted[0]
        for b in range(1, 5):
            part = part + taps[5 * a + b] * shifted[b]
        if a != 2:
            part = pltpu.roll(part, (2 - a) % n, 0)
        part = part[first : first + count]
        total = part if total is None else total + part
    return total


def kernel(
    sections,
    tiles,
    image,
    weight,
    anchor,
    tables,
    taps_ref,
    src_ref,
    dst_ref,
    valid_ref,
    out,
    img,
    wgt,
    halo,
    out_mid,
    out_edge,
    in_mid,
    in_edge,
    strip_mid,
    strip_edge,
    pre_mid,
    pre_edge,
    spec,
    tab,
    load_sem,
    halo_send,
    halo_recv,
    mid_send,
    mid_recv,
    edge_send,
    edge_recv,
    strip_send,
    strip_recv,
):
    sec = lax.axis_index("sec")
    me = lax.axis_index("tile")
    th, tw = image.shape[1:]
    side = wgt.shape[1]
    blocks = strip_mid.shape[0] - 1
    cap = in_mid.shape[1]
    across, down = tw // side, th // side
    padded = across + 2
    mid = side - 2 * EDGE

    barrier = pltpu.get_barrier_semaphore()

    def greet(target):
        pl.semaphore_signal(barrier, inc=1, device_id=target, device_id_type=MESH)

    for k in range(1, tiles):
        greet((sec, lax.rem(me + k, tiles)))
    has_next, has_prev = sec < sections - 1, sec > 0
    not_first, not_last = me > 0, me < tiles - 1

    @pl.when(has_next)
    def _():
        greet((sec + 1, me))

    @pl.when(has_next & not_first)
    def _():
        greet((sec + 1, me - 1))

    @pl.when(has_prev)
    def _():
        greet((sec - 1, me))

    @pl.when(has_prev & not_last)
    def _():
        greet((sec - 1, me + 1))

    loads = []
    for r in range(down):
        low, high = max(0, r * side - EDGE), min(th, (r + 1) * side + EDGE)
        place = low - (r * side - EDGE)
        for c in range(across):
            columns = pl.ds(c * side, side)
            loads.append(
                pltpu.make_async_copy(
                    image.at[0, pl.ds(low, high - low), columns],
                    img.at[r * padded + c + 1, pl.ds(place, high - low)],
                    load_sem.at[len(loads)],
                )
            )
            loads.append(
                pltpu.make_async_copy(
                    weight.at[0, pl.ds(r * side, side), columns],
                    wgt.at[r * across + c],
                    load_sem.at[len(loads)],
                )
            )
    table_load = pltpu.make_async_copy(tables, tab, load_sem.at[len(loads)])
    for load in loads:
        load.start()
    table_load.start()

    own = pl.ds(0, blocks)
    inner, upper, lower = pl.ds(EDGE, mid), pl.ds(0, EDGE), pl.ds(side - EDGE, EDGE)
    anchor_loads = [
        pltpu.make_async_copy(anchor.at[:, inner], pre_mid.at[own], load_sem.at[len(loads) + 1]),
        pltpu.make_async_copy(
            anchor.at[:, upper], pre_edge.at[own, pl.ds(0, EDGE)], load_sem.at[len(loads) + 2]
        ),
        pltpu.make_async_copy(
            anchor.at[:, lower], pre_edge.at[own, pl.ds(EDGE, EDGE)], load_sem.at[len(loads) + 3]
        ),
    ]

    @pl.when(sec == 0)
    def _():
        for load in anchor_loads:
            load.start()

    zeros = jnp.zeros(img.shape[1:], img.dtype)
    for r in range(down):
        img[r * padded] = zeros
        img[(r + 1) * padded - 1] = zeros

    @pl.when(me == 0)
    def _():
        for c in range(across):
            img[c + 1, :EDGE] = zeros[:EDGE]

    @pl.when(me == tiles - 1)
    def _():
        for c in range(across):
            img[(down - 1) * padded + c + 1, EDGE + side :] = zeros[:EDGE]
        for ref in (strip_mid, strip_edge, pre_mid, pre_edge):
            ref[blocks] = jnp.zeros(ref.shape[1:], ref.dtype)

    def remote(src, dst, send, recv, target):
        return pltpu.make_async_remote_copy(
            src_ref=src,
            dst_ref=dst,
            send_sem=send,
            recv_sem=recv,
            device_id=target,
            device_id_type=MESH,
        )

    halo_down = remote(
        image.at[0, pl.ds(th - EDGE, EDGE)],
        halo.at[0],
        halo_send.at[0],
        halo_recv.at[0],
        (sec, lax.rem(me + 1, tiles)),
    )
    halo_up = remote(
        image.at[0, pl.ds(0, EDGE)],
        halo.at[1],
        halo_send.at[1],
        halo_recv.at[1],
        (sec, lax.rem(me + tiles - 1, tiles)),
    )
    before_me = lax.rem(me + tiles - 1, tiles)
    next_sec = lax.rem(sec + 1, sections)
    anchor_rims = [
        remote(anchor.at[0, rows], ref, strip_send.at[n], strip_recv.at[n], (sec, before_me))
        for n, (rows, ref) in enumerate(
            (
                (inner, pre_mid.at[blocks]),
                (upper, pre_edge.at[blocks, pl.ds(0, EDGE)]),
                (lower, pre_edge.at[blocks, pl.ds(EDGE, EDGE)]),
            )
        )
    ]

    def strip_copies(part, strip, pre):
        first = 3 + 3 * part
        return [
            remote(src, dst, strip_send.at[first + n], strip_recv.at[first + n], target)
            for n, (src, dst, target) in enumerate(
                (
                    (strip.at[0], strip.at[blocks], (sec, before_me)),
                    (strip.at[0], pre.at[blocks], (next_sec, before_me)),
                    (strip.at[own], pre.at[own], (next_sec, me)),
                )
            )
        ]

    mid_copies = strip_copies(0, strip_mid, pre_mid)
    edge_copies = strip_copies(1, strip_edge, pre_edge)

    def start_strip(copies):
        @pl.when(has_next)
        def _():
            copies[2].start()

        @pl.when(has_next & not_first)
        def _():
            copies[1].start()

        @pl.when(not_first)
        def _():
            copies[0].start()

    for load in loads:
        load.wait()

    taps = [taps_ref[0, 0, k] for k in range(25)]
    chips = tiles // 2

    def owner(k):
        chip = lax.rem(me // 2 + 1 + k // 2, chips)
        return chip * 2 + lax.rem(me + 1 + k, 2)

    def picked(target, slot, first, count):
        source = src_ref[0, 0, slot, target]
        place = source + 2 * lax.div(source, across)
        rows = [
            img[place + k, first : first + count + 2 * EDGE].astype(jnp.float32) for k in range(3)
        ]
        rows = [part[EDGE - 8 : EDGE + count + 8] for part in rows]
        corrected = lens(rows, taps, 8, count)
        factor = wgt[source, first : first + count].astype(jnp.float32)
        live = jnp.clip(valid_ref[0, 0, target] - slot, 0, 1).astype(jnp.float32)
        return (corrected * factor * live).astype(jnp.bfloat16)

    def mid_copy(k):
        target = owner(k)
        return remote(
            out_mid.at[target], in_mid.at[me], mid_send.at[target], mid_recv.at[me], (sec, target)
        )

    def edge_copy(k):
        target = owner(k)
        return remote(
            out_edge.at[target],
            in_edge.at[me],
            edge_send.at[target],
            edge_recv.at[me],
            (sec, target),
        )

    def fill_mid(k, ref, place):
        for slot in range(cap):
            for piece in range(0, mid, 32):
                ref[place, slot, piece : piece + 32] = picked(owner(k), slot, EDGE + piece, 32)

    def fill_edge(k, ref, place):
        for slot in range(cap):
            ref[place, slot, :EDGE] = picked(owner(k), slot, 0, EDGE)
            ref[place, slot, EDGE:] = picked(owner(k), slot, side - EDGE, EDGE)

    def send_mid(k):
        fill_mid(k, out_mid, owner(k))
        mid_copy(k).start()

    fill_mid(0, out_mid, owner(0))
    after, before = has_next.astype(jnp.int32), has_prev.astype(jnp.int32)
    peers = after * (1 + not_first.astype(jnp.int32)) + before * (1 + not_last.astype(jnp.int32))
    pl.semaphore_wait(barrier, tiles - 1 + peers)

    @pl.when(not_last)
    def _():
        halo_down.start()

    @pl.when(not_first)
    def _():
        halo_up.start()

    @pl.when((sec == 0) & not_first)
    def _():
        for copy in anchor_rims:
            copy.start()

    mid_copy(0).start()
    pl.loop(1, tiles - 1)(send_mid)
    fill_mid(tiles - 1, in_mid, me)

    @pl.when(not_first)
    def _():
        halo_down.wait_recv()
        for c in range(across):
            img[c + 1, :EDGE] = halo[0, :, c * side : (c + 1) * side]

    @pl.when(not_last)
    def _():
        halo_up.wait_recv()
        for c in range(across):
            img[(down - 1) * padded + c + 1, EDGE + side :] = halo[
                1, :, c * side : (c + 1) * side
            ]

    def send_edge(k):
        fill_edge(k, out_edge, owner(k))
        edge_copy(k).start()

    pl.loop(0, tiles - 1)(send_edge)
    fill_edge(tiles - 1, in_edge, me)

    def summed(ref, start, count):
        totals = [None] * blocks
        for t in range(tiles):
            for slot in range(cap):
                value = ref[t, slot, pl.ds(start, count)].astype(jnp.float32)
                place = dst_ref[0, 0, slot, t]
                for j in range(blocks):
                    term = value * (1 - jnp.minimum(jnp.abs(place - j), 1)).astype(jnp.float32)
                    totals[j] = term if totals[j] is None else totals[j] + term
        return [total.astype(jnp.bfloat16) for total in totals]

    def arrive(copy_of):
        def step(k):
            source = owner(k)
            copy_of(k, source).wait_recv()

        return step

    def mid_from(k, source):
        return remote(
            out_mid.at[source], in_mid.at[source], mid_send.at[source], mid_recv.at[source], (sec, source)
        )

    def edge_from(k, source):
        return remote(
            out_edge.at[source], in_edge.at[source], edge_send.at[source], edge_recv.at[source], (sec, source)
        )

    repeat(tiles - 1, arrive(mid_from))
    for piece in range(0, mid, 32):
        for j, value in enumerate(summed(in_mid, piece, 32)):
            strip_mid[j, piece : piece + 32] = value
    start_strip(mid_copies)
    repeat(tiles - 1, arrive(edge_from))
    for j, value in enumerate(summed(in_edge, 0, 2 * EDGE)):
        strip_edge[j] = value
    start_strip(edge_copies)

    table_load.wait()
    right_table = tab.at[pl.ds(0, 2 * side)]
    left_table = tab.at[pl.ds(2 * side, 2 * side)]

    def whole(mid_ref, edge_ref, m):
        edge = edge_ref[m]
        return jnp.concatenate([edge[:EDGE], mid_ref[m], edge[EDGE:]], 0)

    def spectra(mid_ref, edge_ref, m):
        block, after = whole(mid_ref, edge_ref, m), whole(mid_ref, edge_ref, m + 1)
        lane = lax.broadcasted_iota(jnp.int32, block.shape, 1)
        shifted = jnp.where(
            lane < side // 2, after.astype(jnp.float32), block.astype(jnp.float32)
        ).astype(block.dtype)
        windows = jnp.concatenate([block, shifted], 0)
        right = jnp.dot(
            windows, right_table[:side], preferred_element_type=jnp.float32
        ).astype(jnp.bfloat16)
        stacked = jnp.concatenate(
            [
                jnp.concatenate([right[:side, :side], right[:side, side:]], 0),
                jnp.concatenate([right[side:, :side], right[side:, side:]], 0),
            ],
            1,
        )
        return jnp.dot(left_table[...], stacked, preferred_element_type=jnp.float32)

    def keep(m):
        spec[m] = spectra(strip_mid, strip_edge, m)

    repeat(blocks - 1, keep)

    @pl.when(not_last)
    def _():
        mid_copies[0].wait_recv()
        edge_copies[0].wait_recv()

    keep(blocks - 1)

    @pl.when(has_prev)
    def _():
        mid_copies[2].wait_recv()
        edge_copies[2].wait_recv()

    @pl.when(has_prev & not_last)
    def _():
        mid_copies[1].wait_recv()
        edge_copies[1].wait_recv()

    @pl.when(sec == 0)
    def _():
        for load in anchor_loads:
            load.wait()

    @pl.when((sec == 0) & not_last)
    def _():
        for copy in anchor_rims:
            copy.wait_recv()

    def correlate(m):
        earlier = spectra(pre_mid, pre_edge, m)
        current = spec[m]
        cur_re, cur_im = current[:side], current[side:]
        pre_re, pre_im = earlier[:side], earlier[side:]
        cross_re = cur_re * pre_re + cur_im * pre_im
        cross_im = cur_im * pre_re - cur_re * pre_im
        magnitude = jnp.sqrt(cross_re * cross_re + cross_im * cross_im)
        whitened = []
        for half in range(2):
            cols = slice(half * side, (half + 1) * side)
            mag = magnitude[:, cols]
            mean = jnp.sum(mag) * (1.0 / (side * side))
            scale = (1.0 / side) / (mag + (0.1 * mean + 1e-06))
            whitened.append(
                jnp.concatenate([cross_re[:, cols] * scale, cross_im[:, cols] * scale], 1)
            )
        whitened = jnp.concatenate(whitened, 0).astype(jnp.bfloat16)
        rows = jnp.dot(
            whitened, right_table[...], preferred_element_type=jnp.float32
        ).astype(jnp.bfloat16)
        stacked = jnp.concatenate(
            [
                jnp.concatenate([rows[:side, :side], rows[:side, side:]], 0),
                jnp.concatenate([rows[side:, :side], rows[side:, side:]], 0),
            ],
            1,
        )
        result = jnp.dot(left_table[:side], stacked, preferred_element_type=jnp.float32)
        out[0, 2 * m] = result[:, :side]
        out[0, 2 * m + 1] = result[:, side:]

    repeat(blocks, correlate)

    @pl.when(not_last)
    def _():
        halo_down.wait_send()

    @pl.when(not_first)
    def _():
        halo_up.wait_send()
        mid_copies[0].wait_send()
        edge_copies[0].wait_send()

    @pl.when((sec == 0) & not_first)
    def _():
        for copy in anchor_rims:
            copy.wait_send()

    @pl.when(has_next)
    def _():
        mid_copies[2].wait_send()
        edge_copies[2].wait_send()

    @pl.when(has_next & not_first)
    def _():
        mid_copies[1].wait_send()
        edge_copies[1].wait_send()

    def left_here(k):
        mid_copy(k).wait_send()
        edge_copy(k).wait_send()

    repeat(tiles - 1, left_here)


def solution(mesh):
    sections, tiles = mesh.shape["sec"], mesh.shape["tile"]

    def body(image, weight, lens_filter_taps, block_src, block_dst, valid_count, anchor):
        th, tw = image.shape[1:]
        blocks, side = anchor.shape[:2]
        cap = block_src.shape[-1]
        anywhere = pl.BlockSpec(memory_space=pl.ANY)
        scalars = pl.BlockSpec(memory_space=pltpu.SMEM)
        bf16 = jnp.bfloat16
        dma = pltpu.SemaphoreType.DMA
        mid = side - 2 * EDGE
        across, down = tw // side, th // side
        return pl.pallas_call(
            functools.partial(kernel, sections, tiles),
            out_shape=jax.ShapeDtypeStruct((1, 2 * blocks, side, side), jnp.float32),
            in_specs=[anywhere] * 4 + [scalars] * 4,
            out_specs=pl.BlockSpec(memory_space=pltpu.VMEM),
            scratch_shapes=[
                pltpu.VMEM((down * (across + 2), side + 2 * EDGE, side), bf16),
                pltpu.VMEM((down * across, side, side), bf16),
                pltpu.VMEM((2, EDGE, tw), bf16),
                pltpu.VMEM((tiles, cap, mid, side), bf16),
                pltpu.VMEM((tiles, cap, 2 * EDGE, side), bf16),
                pltpu.VMEM((tiles, cap, mid, side), bf16),
                pltpu.VMEM((tiles, cap, 2 * EDGE, side), bf16),
                pltpu.VMEM((blocks + 1, mid, side), bf16),
                pltpu.VMEM((blocks + 1, 2 * EDGE, side), bf16),
                pltpu.VMEM((blocks + 1, mid, side), bf16),
                pltpu.VMEM((blocks + 1, 2 * EDGE, side), bf16),
                pltpu.VMEM((blocks, 2 * side, 2 * side), jnp.float32),
                pltpu.VMEM((4 * side, 2 * side), bf16),
                dma((2 * down * across + 4,)),
                dma((2,)),
                dma((2,)),
                dma((tiles,)),
                dma((tiles,)),
                dma((tiles,)),
                dma((tiles,)),
                dma((9,)),
                dma((9,)),
            ],
            compiler_params=pltpu.CompilerParams(collective_id=0, has_side_effects=True),
        )(
            image,
            weight,
            anchor,
            dft_tables(side),
            lens_filter_taps,
            block_src.transpose(0, 1, 3, 2),
            block_dst.transpose(0, 2, 3, 1),
            valid_count,
        )

    in_specs = (
        P("sec", "tile", None),
        P("sec", "tile", None),
        P("sec", "tile", None),
        P("sec", "tile", None, None),
        P("sec", None, "tile", None),
        P("sec", "tile", None),
        P("tile", None, None),
    )
    out_specs = P("sec", "tile", None, None)
    return jax.shard_map(body, mesh=mesh, in_specs=in_specs, out_specs=out_specs, check_vma=False)
```

```python
import functools
import math

import jax
import jax.numpy as jnp
import numpy as np
from jax import lax
from jax.experimental import pallas as pl
from jax.experimental.pallas import tpu as pltpu
from jax.sharding import PartitionSpec as P

MESH = pl.DeviceIdType.MESH
EDGE = 16
LANES = 128


def repeat(count, step):
    if count <= 4:
        for i in range(count):
            step(i)
    else:
        pl.loop(0, count)(step)


def dft_tables(size):
    positions = np.arange(size)
    angle = (positions[:, None] * positions[None, :] % size) * (2.0 * math.pi / size)
    cosine, sine = np.cos(angle), np.sin(angle)
    inverse_right = np.block([[cosine, sine], [-sine, cosine]])
    forward_left = np.block([[cosine, -sine], [-sine, -cosine]])
    return jnp.asarray(np.concatenate([inverse_right, forward_left], 0), jnp.bfloat16)


def lens(rows, taps, first, count):
    left, middle, right = rows
    lane = lax.broadcasted_iota(jnp.int32, middle.shape, 1)
    shifted = []
    for off in range(-2, 3):
        if off == 0:
            shifted.append(middle)
        elif off > 0:
            mixed = jnp.where(lane < off, right, middle)
            shifted.append(pltpu.roll(mixed, LANES - off, 1))
        else:
            mixed = jnp.where(lane >= LANES + off, left, middle)
            shifted.append(pltpu.roll(mixed, -off, 1))
    total = None
    n = middle.shape[0]
    for a in range(5):
        part = taps[5 * a] * shifted[0]
        for b in range(1, 5):
            part = part + taps[5 * a + b] * shifted[b]
        if a != 2:
            part = pltpu.roll(part, (2 - a) % n, 0)
        part = part[first : first + count]
        total = part if total is None else total + part
    return total


def kernel(
    sections,
    tiles,
    image,
    weight,
    anchor,
    tables,
    taps_any,
    src_any,
    dst_any,
    valid_any,
    out,
    taps_ref,
    src_ref,
    dst_ref,
    valid_ref,
    img,
    wgt,
    halo,
    out_mid,
    out_edge,
    in_mid,
    in_edge,
    strip_mid,
    strip_edge,
    pre_mid,
    pre_edge,
    spec,
    tab,
    load_sem,
    halo_send,
    halo_recv,
    mid_send,
    mid_recv,
    edge_send,
    edge_recv,
    strip_send,
    strip_recv,
    anchor_send,
):
    sec = lax.axis_index("sec")
    me = lax.axis_index("tile")
    th, tw = image.shape[1:]
    side = wgt.shape[1]
    blocks = strip_mid.shape[0] - 1
    cap = in_mid.shape[1]
    across, down = tw // side, th // side
    padded = across + 2
    mid = side - 2 * EDGE

    barrier = pltpu.get_barrier_semaphore()

    def greet(target):
        pl.semaphore_signal(barrier, inc=1, device_id=target, device_id_type=MESH)

    for k in range(1, tiles):
        greet((sec, lax.rem(me + k, tiles)))
    has_next, has_prev = sec < sections - 1, sec > 0
    not_first, not_last = me > 0, me < tiles - 1

    @pl.when(has_next)
    def _():
        greet((sec + 1, me))

    @pl.when(has_next & not_first)
    def _():
        greet((sec + 1, me - 1))

    @pl.when(has_prev)
    def _():
        greet((sec - 1, me))

    @pl.when(has_prev & not_last)
    def _():
        greet((sec - 1, me + 1))

    loads = []
    for source, ref in (
        (taps_any, taps_ref),
        (src_any, src_ref),
        (dst_any, dst_ref),
        (valid_any, valid_ref),
    ):
        loads.append(pltpu.make_async_copy(source, ref, load_sem.at[len(loads)]))
    for r in range(down):
        low, high = max(0, r * side - EDGE), min(th, (r + 1) * side + EDGE)
        place = low - (r * side - EDGE)
        for c in range(across):
            columns = pl.ds(c * side, side)
            loads.append(
                pltpu.make_async_copy(
                    image.at[0, pl.ds(low, high - low), columns],
                    img.at[r * padded + c + 1, pl.ds(place, high - low)],
                    load_sem.at[len(loads)],
                )
            )
            loads.append(
                pltpu.make_async_copy(
                    weight.at[0, pl.ds(r * side, side), columns],
                    wgt.at[r * across + c],
                    load_sem.at[len(loads)],
                )
            )
    table_load = pltpu.make_async_copy(tables, tab, load_sem.at[len(loads)])
    for load in loads:
        load.start()
    table_load.start()

    inner, upper, lower = pl.ds(EDGE, mid), pl.ds(0, EDGE), pl.ds(side - EDGE, EDGE)
    rim_at = 2 * blocks

    def anchor_load(j):
        for rows, ref, at in (
            (inner, pre_mid.at[j], 2 * j),
            (upper, pre_edge.at[j, pl.ds(0, EDGE)], 2 * j + 1),
            (lower, pre_edge.at[j, pl.ds(EDGE, EDGE)], 2 * j + 1),
        ):
            pltpu.make_async_copy(anchor.at[j, rows], ref, strip_recv.at[at]).start()

    @pl.when(sec == 0)
    def _():
        repeat(blocks, anchor_load)

    zeros = jnp.zeros(img.shape[1:], img.dtype)
    for r in range(down):
        img[r * padded] = zeros
        img[(r + 1) * padded - 1] = zeros

    @pl.when(me == 0)
    def _():
        for c in range(across):
            img[c + 1, :EDGE] = zeros[:EDGE]

    @pl.when(me == tiles - 1)
    def _():
        for c in range(across):
            img[(down - 1) * padded + c + 1, EDGE + side :] = zeros[:EDGE]
        for ref in (strip_mid, strip_edge, pre_mid, pre_edge):
            ref[blocks] = jnp.zeros(ref.shape[1:], ref.dtype)

    def remote(src, dst, send, recv, target):
        return pltpu.make_async_remote_copy(
            src_ref=src,
            dst_ref=dst,
            send_sem=send,
            recv_sem=recv,
            device_id=target,
            device_id_type=MESH,
        )

    halo_down = remote(
        image.at[0, pl.ds(th - EDGE, EDGE)],
        halo.at[0],
        halo_send.at[0],
        halo_recv.at[0],
        (sec, lax.rem(me + 1, tiles)),
    )
    halo_up = remote(
        image.at[0, pl.ds(0, EDGE)],
        halo.at[1],
        halo_send.at[1],
        halo_recv.at[1],
        (sec, lax.rem(me + tiles - 1, tiles)),
    )
    before_me = lax.rem(me + tiles - 1, tiles)
    next_sec = lax.rem(sec + 1, sections)
    anchor_rims = [
        remote(anchor.at[0, rows], ref, anchor_send.at[n], strip_recv.at[at], (sec, before_me))
        for n, (rows, ref, at) in enumerate(
            (
                (inner, pre_mid.at[blocks], rim_at),
                (upper, pre_edge.at[blocks, pl.ds(0, EDGE)], rim_at + 1),
                (lower, pre_edge.at[blocks, pl.ds(EDGE, EDGE)], rim_at + 1),
            )
        )
    ]
    parts = ((strip_mid, pre_mid), (strip_edge, pre_edge))

    def onward(part, j):
        strip, pre = parts[part]
        at = 2 * j + part
        return remote(strip.at[j], pre.at[j], strip_send.at[at], strip_recv.at[at], (next_sec, me))

    def onward_rim(part):
        strip, pre = parts[part]
        at = rim_at + part
        return remote(
            strip.at[0], pre.at[blocks], strip_send.at[at], strip_recv.at[at], (next_sec, before_me)
        )

    def own_rim(part):
        strip, _ = parts[part]
        at = rim_at + 2 + part
        return remote(
            strip.at[0], strip.at[blocks], strip_send.at[at], strip_recv.at[at], (sec, before_me)
        )

    def start_rims(part):
        @pl.when(has_next & not_first)
        def _():
            onward_rim(part).start()

        @pl.when(not_first)
        def _():
            own_rim(part).start()

    ahead = min(2, blocks)

    for load in loads:
        load.wait()

    taps = [taps_ref[0, 0, k] for k in range(25)]
    chips = tiles // 2

    def owner(k):
        chip = lax.rem(me // 2 + 1 + k // 2, chips)
        return chip * 2 + lax.rem(me + 1 + k, 2)

    def picked(target, slot, first, count):
        source = src_ref[0, 0, slot, target]
        place = source + 2 * lax.div(source, across)
        rows = [
            img[place + k, first : first + count + 2 * EDGE].astype(jnp.float32) for k in range(3)
        ]
        rows = [part[EDGE - 8 : EDGE + count + 8] for part in rows]
        corrected = lens(rows, taps, 8, count)
        factor = wgt[source, first : first + count].astype(jnp.float32)
        live = jnp.clip(valid_ref[0, 0, target] - slot, 0, 1).astype(jnp.float32)
        return (corrected * factor * live).astype(jnp.bfloat16)

    def mid_copy(k):
        target = owner(k)
        return remote(
            out_mid.at[target], in_mid.at[me], mid_send.at[target], mid_recv.at[me], (sec, target)
        )

    def edge_copy(k):
        target = owner(k)
        return remote(
            out_edge.at[target],
            in_edge.at[me],
            edge_send.at[target],
            edge_recv.at[me],
            (sec, target),
        )

    def fill_mid(k, ref, place):
        for slot in range(cap):
            for piece in range(0, mid, 32):
                ref[place, slot, piece : piece + 32] = picked(owner(k), slot, EDGE + piece, 32)

    def fill_edge(k, ref, place):
        for slot in range(cap):
            ref[place, slot, :EDGE] = picked(owner(k), slot, 0, EDGE)
            ref[place, slot, EDGE:] = picked(owner(k), slot, side - EDGE, EDGE)

    def send_mid(k):
        fill_mid(k, out_mid, owner(k))
        mid_copy(k).start()

    fill_mid(0, out_mid, owner(0))
    after, before = has_next.astype(jnp.int32), has_prev.astype(jnp.int32)
    peers = after * (1 + not_first.astype(jnp.int32)) + before * (1 + not_last.astype(jnp.int32))
    pl.semaphore_wait(barrier, tiles - 1 + peers)

    @pl.when(not_last)
    def _():
        halo_down.start()

    @pl.when(not_first)
    def _():
        halo_up.start()

    @pl.when((sec == 0) & not_first)
    def _():
        for copy in anchor_rims:
            copy.start()

    mid_copy(0).start()
    pl.loop(1, tiles - 1)(send_mid)
    fill_mid(tiles - 1, in_mid, me)

    @pl.when(not_first)
    def _():
        halo_down.wait_recv()
        for c in range(across):
            img[c + 1, :EDGE] = halo[0, :, c * side : (c + 1) * side]

    @pl.when(not_last)
    def _():
        halo_up.wait_recv()
        for c in range(across):
            img[(down - 1) * padded + c + 1, EDGE + side :] = halo[
                1, :, c * side : (c + 1) * side
            ]

    def send_edge(k):
        fill_edge(k, out_edge, owner(k))
        edge_copy(k).start()

    pl.loop(0, tiles - 1)(send_edge)
    fill_edge(tiles - 1, in_edge, me)

    def summed(ref, start, count):
        totals = [None] * blocks
        for t in range(tiles):
            for slot in range(cap):
                value = ref[t, slot, pl.ds(start, count)].astype(jnp.float32)
                place = dst_ref[0, 0, slot, t]
                for j in range(blocks):
                    term = value * (1 - jnp.minimum(jnp.abs(place - j), 1)).astype(jnp.float32)
                    totals[j] = term if totals[j] is None else totals[j] + term
        return [total.astype(jnp.bfloat16) for total in totals]

    def arrive(copy_of):
        def step(k):
            source = owner(k)
            copy_of(k, source).wait_recv()

        return step

    def mid_from(k, source):
        return remote(
            out_mid.at[source], in_mid.at[source], mid_send.at[source], mid_recv.at[source], (sec, source)
        )

    def edge_from(k, source):
        return remote(
            out_edge.at[source], in_edge.at[source], edge_send.at[source], edge_recv.at[source], (sec, source)
        )

    repeat(tiles - 1, arrive(mid_from))
    for piece in range(0, mid, 32):
        for j, value in enumerate(summed(in_mid, piece, 32)):
            strip_mid[j, piece : piece + 32] = value
    start_rims(0)

    @pl.when(has_next)
    def _():
        for j in range(ahead):
            onward(0, blocks - 1 - j).start()

    repeat(tiles - 1, arrive(edge_from))
    for j, value in enumerate(summed(in_edge, 0, 2 * EDGE)):
        strip_edge[j] = value
    start_rims(1)

    @pl.when(has_next)
    def _():
        for j in range(ahead):
            onward(1, blocks - 1 - j).start()

        def later(k):
            j = blocks - 1 - ahead - k
            onward(0, j).start()
            onward(1, j).start()

        repeat(blocks - ahead, later)


    table_load.wait()
    right_table = tab.at[pl.ds(0, 2 * side)]
    left_table = tab.at[pl.ds(2 * side, 2 * side)]

    def whole(mid_ref, edge_ref, m):
        edge = edge_ref[m]
        return jnp.concatenate([edge[:EDGE], mid_ref[m], edge[EDGE:]], 0)

    def spectra(mid_ref, edge_ref, m):
        block, after = whole(mid_ref, edge_ref, m), whole(mid_ref, edge_ref, m + 1)
        lane = lax.broadcasted_iota(jnp.int32, block.shape, 1)
        shifted = jnp.where(
            lane < side // 2, after.astype(jnp.float32), block.astype(jnp.float32)
        ).astype(block.dtype)
        windows = jnp.concatenate([block, shifted], 0)
        right = jnp.dot(
            windows, right_table[:side], preferred_element_type=jnp.float32
        ).astype(jnp.bfloat16)
        stacked = jnp.concatenate(
            [
                jnp.concatenate([right[:side, :side], right[:side, side:]], 0),
                jnp.concatenate([right[side:, :side], right[side:, side:]], 0),
            ],
            1,
        )
        return jnp.dot(left_table[...], stacked, preferred_element_type=jnp.float32)

    def keep(m):
        spec[m] = spectra(strip_mid, strip_edge, m)

    repeat(blocks - 1, keep)

    @pl.when(not_last)
    def _():
        own_rim(0).wait_recv()
        own_rim(1).wait_recv()

    keep(blocks - 1)

    @pl.when(not_last)
    def _():
        onward_rim(0).wait_recv()
        onward_rim(1).wait_recv()

    def correlate(k):
        m = blocks - 1 - k
        onward(0, m).wait_recv()
        onward(1, m).wait_recv()
        earlier = spectra(pre_mid, pre_edge, m)
        current = spec[m]
        cur_re, cur_im = current[:side], current[side:]
        pre_re, pre_im = earlier[:side], earlier[side:]
        cross_re = cur_re * pre_re + cur_im * pre_im
        cross_im = cur_im * pre_re - cur_re * pre_im
        magnitude = jnp.sqrt(cross_re * cross_re + cross_im * cross_im)
        whitened = []
        for half in range(2):
            cols = slice(half * side, (half + 1) * side)
            mag = magnitude[:, cols]
            mean = jnp.sum(mag) * (1.0 / (side * side))
            scale = (1.0 / side) / (mag + (0.1 * mean + 1e-06))
            whitened.append(
                jnp.concatenate([cross_re[:, cols] * scale, cross_im[:, cols] * scale], 1)
            )
        whitened = jnp.concatenate(whitened, 0).astype(jnp.bfloat16)
        rows = jnp.dot(
            whitened, right_table[...], preferred_element_type=jnp.float32
        ).astype(jnp.bfloat16)
        stacked = jnp.concatenate(
            [
                jnp.concatenate([rows[:side, :side], rows[:side, side:]], 0),
                jnp.concatenate([rows[side:, :side], rows[side:, side:]], 0),
            ],
            1,
        )
        result = jnp.dot(left_table[:side], stacked, preferred_element_type=jnp.float32)
        out[0, 2 * m] = result[:, :side]
        out[0, 2 * m + 1] = result[:, side:]

    repeat(blocks, correlate)

    @pl.when(not_last)
    def _():
        halo_down.wait_send()

    @pl.when(not_first)
    def _():
        halo_up.wait_send()
        own_rim(0).wait_send()
        own_rim(1).wait_send()

    @pl.when((sec == 0) & not_first)
    def _():
        for copy in anchor_rims:
            copy.wait_send()

    @pl.when(has_next)
    def _():
        def gone(j):
            onward(0, j).wait_send()
            onward(1, j).wait_send()

        repeat(blocks, gone)

    @pl.when(has_next & not_first)
    def _():
        onward_rim(0).wait_send()
        onward_rim(1).wait_send()

    def left_here(k):
        mid_copy(k).wait_send()
        edge_copy(k).wait_send()

    repeat(tiles - 1, left_here)


def solution(mesh):
    sections, tiles = mesh.shape["sec"], mesh.shape["tile"]

    def body(image, weight, lens_filter_taps, block_src, block_dst, valid_count, anchor):
        th, tw = image.shape[1:]
        blocks, side = anchor.shape[:2]
        cap = block_src.shape[-1]
        anywhere = pl.BlockSpec(memory_space=pl.ANY)
        bf16 = jnp.bfloat16
        dma = pltpu.SemaphoreType.DMA
        mid = side - 2 * EDGE
        across, down = tw // side, th // side
        return pl.pallas_call(
            functools.partial(kernel, sections, tiles),
            out_shape=pltpu.VMEM((1, 2 * blocks, side, side), jnp.float32),
            in_specs=[anywhere] * 8,
            out_specs=pl.BlockSpec(memory_space=pltpu.VMEM),
            scratch_shapes=[
                pltpu.SMEM(lens_filter_taps.shape, jnp.float32),
                pltpu.SMEM((1, 1, cap, tiles), jnp.int32),
                pltpu.SMEM((1, 1, cap, tiles), jnp.int32),
                pltpu.SMEM(valid_count.shape, jnp.int32),
                pltpu.VMEM((down * (across + 2), side + 2 * EDGE, side), bf16),
                pltpu.VMEM((down * across, side, side), bf16),
                pltpu.VMEM((2, EDGE, tw), bf16),
                pltpu.VMEM((tiles, cap, mid, side), bf16),
                pltpu.VMEM((tiles, cap, 2 * EDGE, side), bf16),
                pltpu.VMEM((tiles, cap, mid, side), bf16),
                pltpu.VMEM((tiles, cap, 2 * EDGE, side), bf16),
                pltpu.VMEM((blocks + 1, mid, side), bf16),
                pltpu.VMEM((blocks + 1, 2 * EDGE, side), bf16),
                pltpu.VMEM((blocks + 1, mid, side), bf16),
                pltpu.VMEM((blocks + 1, 2 * EDGE, side), bf16),
                pltpu.VMEM((blocks, 2 * side, 2 * side), jnp.float32),
                pltpu.VMEM((4 * side, 2 * side), bf16),
                dma((2 * down * across + 5,)),
                dma((2,)),
                dma((2,)),
                dma((tiles,)),
                dma((tiles,)),
                dma((tiles,)),
                dma((tiles,)),
                dma((2 * blocks + 4,)),
                dma((2 * blocks + 4,)),
                dma((3,)),
            ],
            compiler_params=pltpu.CompilerParams(collective_id=0, has_side_effects=True),
        )(
            image,
            weight,
            anchor,
            dft_tables(side),
            lens_filter_taps,
            block_src.transpose(0, 1, 3, 2),
            block_dst.transpose(0, 2, 3, 1),
            valid_count,
        )

    in_specs = (
        P("sec", "tile", None),
        P("sec", "tile", None),
        P("sec", "tile", None),
        P("sec", "tile", None, None),
        P("sec", None, "tile", None),
        P("sec", "tile", None),
        P("tile", None, None),
    )
    out_specs = P("sec", "tile", None, None)
    return jax.shard_map(body, mesh=mesh, in_specs=in_specs, out_specs=out_specs, check_vma=False)
```

```python
import functools
import math

import jax
import jax.numpy as jnp
import numpy as np
from jax import lax
from jax.experimental import pallas as pl
from jax.experimental.pallas import tpu as pltpu
from jax.sharding import PartitionSpec as P

MESH = pl.DeviceIdType.MESH
EDGE = 16
LANES = 128


def repeat(count, step):
    if count <= 4:
        for i in range(count):
            step(i)
    else:
        pl.loop(0, count)(step)


def dft_tables(size):
    positions = np.arange(size)
    angle = (positions[:, None] * positions[None, :] % size) * (2.0 * math.pi / size)
    cosine, sine = np.cos(angle), np.sin(angle)
    inverse_right = np.block([[cosine, sine], [-sine, cosine]])
    forward_left = np.block([[cosine, -sine], [-sine, -cosine]])
    return jnp.asarray(np.concatenate([inverse_right, forward_left], 0), jnp.bfloat16)


def lens(rows, taps, first, count):
    left, middle, right = rows
    lane = lax.broadcasted_iota(jnp.int32, middle.shape, 1)
    shifted = []
    for off in range(-2, 3):
        if off == 0:
            shifted.append(middle)
        elif off > 0:
            mixed = jnp.where(lane < off, right, middle)
            shifted.append(pltpu.roll(mixed, LANES - off, 1))
        else:
            mixed = jnp.where(lane >= LANES + off, left, middle)
            shifted.append(pltpu.roll(mixed, -off, 1))
    total = None
    n = middle.shape[0]
    for a in range(5):
        part = taps[5 * a] * shifted[0]
        for b in range(1, 5):
            part = part + taps[5 * a + b] * shifted[b]
        if a != 2:
            part = pltpu.roll(part, (2 - a) % n, 0)
        part = part[first : first + count]
        total = part if total is None else total + part
    return total


def kernel(
    sections,
    tiles,
    image,
    weight,
    anchor,
    tables,
    taps_any,
    src_any,
    dst_any,
    valid_any,
    out,
    taps_ref,
    src_ref,
    dst_ref,
    valid_ref,
    img,
    wgt,
    halo,
    out_a,
    out_b,
    out_edge,
    in_a,
    in_b,
    in_edge,
    strip_a,
    strip_b,
    strip_edge,
    pre_a,
    pre_b,
    pre_edge,
    spec,
    tab,
    load_sem,
    halo_send,
    halo_recv,
    block_send,
    block_recv,
    strip_send,
    strip_recv,
    anchor_send,
):
    sec = lax.axis_index("sec")
    me = lax.axis_index("tile")
    th, tw = image.shape[1:]
    side = wgt.shape[1]
    blocks = strip_a.shape[0] - 1
    cap = in_a.shape[1]
    outs, ins = (out_a, out_b, out_edge), (in_a, in_b, in_edge)
    parts = ((strip_a, pre_a), (strip_b, pre_b), (strip_edge, pre_edge))
    count = len(parts)
    across, down = tw // side, th // side
    padded = across + 2
    mid = strip_a.shape[1]

    barrier = pltpu.get_barrier_semaphore()

    def greet(target):
        pl.semaphore_signal(barrier, inc=1, device_id=target, device_id_type=MESH)

    for k in range(1, tiles):
        greet((sec, lax.rem(me + k, tiles)))
    has_next, has_prev = sec < sections - 1, sec > 0
    not_first, not_last = me > 0, me < tiles - 1

    @pl.when(has_next)
    def _():
        greet((sec + 1, me))

    @pl.when(has_next & not_first)
    def _():
        greet((sec + 1, me - 1))

    @pl.when(has_prev)
    def _():
        greet((sec - 1, me))

    @pl.when(has_prev & not_last)
    def _():
        greet((sec - 1, me + 1))

    loads = []
    for source, ref in (
        (taps_any, taps_ref),
        (src_any, src_ref),
        (dst_any, dst_ref),
        (valid_any, valid_ref),
    ):
        loads.append(pltpu.make_async_copy(source, ref, load_sem.at[len(loads)]))
    for r in range(down):
        low, high = max(0, r * side - EDGE), min(th, (r + 1) * side + EDGE)
        place = low - (r * side - EDGE)
        for c in range(across):
            columns = pl.ds(c * side, side)
            loads.append(
                pltpu.make_async_copy(
                    image.at[0, pl.ds(low, high - low), columns],
                    img.at[r * padded + c + 1, pl.ds(place, high - low)],
                    load_sem.at[len(loads)],
                )
            )
            loads.append(
                pltpu.make_async_copy(
                    weight.at[0, pl.ds(r * side, side), columns],
                    wgt.at[r * across + c],
                    load_sem.at[len(loads)],
                )
            )
    table_load = pltpu.make_async_copy(tables, tab, load_sem.at[len(loads)])
    for load in loads:
        load.start()
    table_load.start()

    rim_at = count * blocks

    def anchor_pieces(j):
        return (
            (pl.ds(EDGE, mid), pre_a.at[j], 0),
            (pl.ds(EDGE + mid, mid), pre_b.at[j], 1),
            (pl.ds(0, EDGE), pre_edge.at[j, pl.ds(0, EDGE)], 2),
            (pl.ds(side - EDGE, EDGE), pre_edge.at[j, pl.ds(EDGE, EDGE)], 2),
        )

    def anchor_load(j):
        for rows, ref, part in anchor_pieces(j):
            pltpu.make_async_copy(
                anchor.at[j, rows], ref, strip_recv.at[count * j + part]
            ).start()

    @pl.when(sec == 0)
    def _():
        repeat(blocks, anchor_load)

    zeros = jnp.zeros(img.shape[1:], img.dtype)
    for r in range(down):
        img[r * padded] = zeros
        img[(r + 1) * padded - 1] = zeros

    @pl.when(me == 0)
    def _():
        for c in range(across):
            img[c + 1, :EDGE] = zeros[:EDGE]

    @pl.when(me == tiles - 1)
    def _():
        for c in range(across):
            img[(down - 1) * padded + c + 1, EDGE + side :] = zeros[:EDGE]
        for ref in (strip_a, strip_b, strip_edge, pre_a, pre_b, pre_edge):
            ref[blocks] = jnp.zeros(ref.shape[1:], ref.dtype)

    def remote(src, dst, send, recv, target):
        return pltpu.make_async_remote_copy(
            src_ref=src,
            dst_ref=dst,
            send_sem=send,
            recv_sem=recv,
            device_id=target,
            device_id_type=MESH,
        )

    halo_down = remote(
        image.at[0, pl.ds(th - EDGE, EDGE)],
        halo.at[0],
        halo_send.at[0],
        halo_recv.at[0],
        (sec, lax.rem(me + 1, tiles)),
    )
    halo_up = remote(
        image.at[0, pl.ds(0, EDGE)],
        halo.at[1],
        halo_send.at[1],
        halo_recv.at[1],
        (sec, lax.rem(me + tiles - 1, tiles)),
    )
    before_me = lax.rem(me + tiles - 1, tiles)
    next_sec = lax.rem(sec + 1, sections)
    anchor_rims = [
        remote(
            anchor.at[0, rows],
            ref,
            anchor_send.at[n],
            strip_recv.at[rim_at + part],
            (sec, before_me),
        )
        for n, (rows, ref, part) in enumerate(anchor_pieces(blocks))
    ]

    def onward(part, j):
        strip, pre = parts[part]
        at = count * j + part
        return remote(strip.at[j], pre.at[j], strip_send.at[at], strip_recv.at[at], (next_sec, me))

    def onward_rim(part):
        strip, pre = parts[part]
        at = rim_at + part
        return remote(
            strip.at[0], pre.at[blocks], strip_send.at[at], strip_recv.at[at], (next_sec, before_me)
        )

    def own_rim(part):
        strip, _ = parts[part]
        at = rim_at + count + part
        return remote(
            strip.at[0], strip.at[blocks], strip_send.at[at], strip_recv.at[at], (sec, before_me)
        )

    def start_rims(part):
        @pl.when(has_next & not_first)
        def _():
            onward_rim(part).start()

        @pl.when(not_first)
        def _():
            own_rim(part).start()

    ahead = min(3, blocks)

    for load in loads:
        load.wait()

    taps = [taps_ref[0, 0, k] for k in range(25)]
    chips = tiles // 2

    def owner(k):
        chip = lax.rem(me // 2 + 1 + k // 2, chips)
        return chip * 2 + lax.rem(me + 1 + k, 2)

    def picked(target, slot, first, count):
        source = src_ref[0, 0, slot, target]
        place = source + 2 * lax.div(source, across)
        rows = [
            img[place + k, first : first + count + 2 * EDGE].astype(jnp.float32) for k in range(3)
        ]
        rows = [part[EDGE - 8 : EDGE + count + 8] for part in rows]
        corrected = lens(rows, taps, 8, count)
        factor = wgt[source, first : first + count].astype(jnp.float32)
        live = jnp.clip(valid_ref[0, 0, target] - slot, 0, 1).astype(jnp.float32)
        return (corrected * factor * live).astype(jnp.bfloat16)

    def block_copy(part, k):
        target = owner(k)
        return remote(
            outs[part].at[target],
            ins[part].at[me],
            block_send.at[part, target],
            block_recv.at[part, me],
            (sec, target),
        )

    def block_from(part, k):
        source = owner(k)
        return remote(
            outs[part].at[source],
            ins[part].at[source],
            block_send.at[part, source],
            block_recv.at[part, source],
            (sec, source),
        )

    def fill(part, k, ref, place):
        for slot in range(cap):
            if part < count - 1:
                ref[place, slot] = picked(owner(k), slot, EDGE + part * mid, mid)
            else:
                ref[place, slot, :EDGE] = picked(owner(k), slot, 0, EDGE)
                ref[place, slot, EDGE:] = picked(owner(k), slot, side - EDGE, EDGE)

    def send(part, first, last):
        def step(k):
            fill(part, k, outs[part], owner(k))
            block_copy(part, k).start()

        pl.loop(first, last)(step)

    far = tiles - 2
    fill(0, 0, out_a, owner(0))
    after, before = has_next.astype(jnp.int32), has_prev.astype(jnp.int32)
    peers = after * (1 + not_first.astype(jnp.int32)) + before * (1 + not_last.astype(jnp.int32))
    pl.semaphore_wait(barrier, tiles - 1 + peers)

    @pl.when(not_last)
    def _():
        halo_down.start()

    @pl.when(not_first)
    def _():
        halo_up.start()

    @pl.when((sec == 0) & not_first)
    def _():
        for copy in anchor_rims:
            copy.start()

    block_copy(0, 0).start()
    send(0, 1, far)
    send(1, 0, far)
    send(0, far, tiles - 1)
    send(1, far, tiles - 1)
    fill(0, tiles - 1, in_a, me)
    fill(1, tiles - 1, in_b, me)

    @pl.when(not_first)
    def _():
        halo_down.wait_recv()
        for c in range(across):
            img[c + 1, :EDGE] = halo[0, :, c * side : (c + 1) * side]

    @pl.when(not_last)
    def _():
        halo_up.wait_recv()
        for c in range(across):
            img[(down - 1) * padded + c + 1, EDGE + side :] = halo[
                1, :, c * side : (c + 1) * side
            ]

    send(2, 0, tiles - 1)
    fill(2, tiles - 1, in_edge, me)

    def add_up(part):
        repeat(tiles - 1, lambda k: block_from(part, k).wait_recv())
        totals = [None] * blocks
        for t in range(tiles):
            for slot in range(cap):
                value = ins[part][t, slot].astype(jnp.float32)
                place = dst_ref[0, 0, slot, t]
                for j in range(blocks):
                    term = value * (1 - jnp.minimum(jnp.abs(place - j), 1)).astype(jnp.float32)
                    totals[j] = term if totals[j] is None else totals[j] + term
        for j, total in enumerate(totals):
            parts[part][0][j] = total.astype(jnp.bfloat16)
        start_rims(part)

        @pl.when(has_next)
        def _():
            for k in range(ahead):
                onward(part, blocks - 1 - k).start()

    for part in range(count):
        add_up(part)

    @pl.when(has_next)
    def _():
        def later(k):
            for part in range(count):
                onward(part, blocks - 1 - ahead - k).start()

        repeat(blocks - ahead, later)

    table_load.wait()
    right_table = tab.at[pl.ds(0, 2 * side)]
    left_table = tab.at[pl.ds(2 * side, 2 * side)]

    def whole(which, m):
        first, second, edge = (pair[which][m] for pair in parts)
        return jnp.concatenate([edge[:EDGE], first, second, edge[EDGE:]], 0)

    def spectra(which, m):
        block, after = whole(which, m), whole(which, m + 1)
        lane = lax.broadcasted_iota(jnp.int32, block.shape, 1)
        shifted = jnp.where(
            lane < side // 2, after.astype(jnp.float32), block.astype(jnp.float32)
        ).astype(block.dtype)
        windows = jnp.concatenate([block, shifted], 0)
        right = jnp.dot(
            windows, right_table[:side], preferred_element_type=jnp.float32
        ).astype(jnp.bfloat16)
        stacked = jnp.concatenate(
            [
                jnp.concatenate([right[:side, :side], right[:side, side:]], 0),
                jnp.concatenate([right[side:, :side], right[side:, side:]], 0),
            ],
            1,
        )
        return jnp.dot(left_table[...], stacked, preferred_element_type=jnp.float32)

    def keep(m):
        spec[m] = spectra(0, m)

    repeat(blocks - 1, keep)

    @pl.when(not_last)
    def _():
        for part in range(count):
            own_rim(part).wait_recv()

    keep(blocks - 1)

    @pl.when(not_last)
    def _():
        for part in range(count):
            onward_rim(part).wait_recv()

    def correlate(k):
        m = blocks - 1 - k
        for part in range(count):
            onward(part, m).wait_recv()
        earlier = spectra(1, m)
        current = spec[m]
        cur_re, cur_im = current[:side], current[side:]
        pre_re, pre_im = earlier[:side], earlier[side:]
        cross_re = cur_re * pre_re + cur_im * pre_im
        cross_im = cur_im * pre_re - cur_re * pre_im
        magnitude = jnp.sqrt(cross_re * cross_re + cross_im * cross_im)
        whitened = []
        for half in range(2):
            cols = slice(half * side, (half + 1) * side)
            mag = magnitude[:, cols]
            mean = jnp.sum(mag) * (1.0 / (side * side))
            scale = (1.0 / side) / (mag + (0.1 * mean + 1e-06))
            whitened.append(
                jnp.concatenate([cross_re[:, cols] * scale, cross_im[:, cols] * scale], 1)
            )
        whitened = jnp.concatenate(whitened, 0).astype(jnp.bfloat16)
        rows = jnp.dot(
            whitened, right_table[...], preferred_element_type=jnp.float32
        ).astype(jnp.bfloat16)
        stacked = jnp.concatenate(
            [
                jnp.concatenate([rows[:side, :side], rows[:side, side:]], 0),
                jnp.concatenate([rows[side:, :side], rows[side:, side:]], 0),
            ],
            1,
        )
        result = jnp.dot(left_table[:side], stacked, preferred_element_type=jnp.float32)
        out[0, 2 * m] = result[:, :side]
        out[0, 2 * m + 1] = result[:, side:]

    repeat(blocks, correlate)

    @pl.when(not_last)
    def _():
        halo_down.wait_send()

    @pl.when(not_first)
    def _():
        halo_up.wait_send()
        for part in range(count):
            own_rim(part).wait_send()

    @pl.when((sec == 0) & not_first)
    def _():
        for copy in anchor_rims:
            copy.wait_send()

    @pl.when(has_next)
    def _():
        def gone(j):
            for part in range(count):
                onward(part, j).wait_send()

        repeat(blocks, gone)

    @pl.when(has_next & not_first)
    def _():
        for part in range(count):
            onward_rim(part).wait_send()

    def left_here(k):
        for part in range(count):
            block_copy(part, k).wait_send()

    repeat(tiles - 1, left_here)


def solution(mesh):
    sections, tiles = mesh.shape["sec"], mesh.shape["tile"]

    def body(image, weight, lens_filter_taps, block_src, block_dst, valid_count, anchor):
        th, tw = image.shape[1:]
        blocks, side = anchor.shape[:2]
        cap = block_src.shape[-1]
        anywhere = pl.BlockSpec(memory_space=pl.ANY)
        bf16 = jnp.bfloat16
        dma = pltpu.SemaphoreType.DMA
        mid = (side - 2 * EDGE) // 2
        across, down = tw // side, th // side
        return pl.pallas_call(
            functools.partial(kernel, sections, tiles),
            out_shape=pltpu.VMEM((1, 2 * blocks, side, side), jnp.float32),
            in_specs=[anywhere] * 8,
            out_specs=pl.BlockSpec(memory_space=pltpu.VMEM),
            scratch_shapes=[
                pltpu.SMEM(lens_filter_taps.shape, jnp.float32),
                pltpu.SMEM((1, 1, cap, tiles), jnp.int32),
                pltpu.SMEM((1, 1, cap, tiles), jnp.int32),
                pltpu.SMEM(valid_count.shape, jnp.int32),
                pltpu.VMEM((down * (across + 2), side + 2 * EDGE, side), bf16),
                pltpu.VMEM((down * across, side, side), bf16),
                pltpu.VMEM((2, EDGE, tw), bf16),
                pltpu.VMEM((tiles, cap, mid, side), bf16),
                pltpu.VMEM((tiles, cap, mid, side), bf16),
                pltpu.VMEM((tiles, cap, 2 * EDGE, side), bf16),
                pltpu.VMEM((tiles, cap, mid, side), bf16),
                pltpu.VMEM((tiles, cap, mid, side), bf16),
                pltpu.VMEM((tiles, cap, 2 * EDGE, side), bf16),
                pltpu.VMEM((blocks + 1, mid, side), bf16),
                pltpu.VMEM((blocks + 1, mid, side), bf16),
                pltpu.VMEM((blocks + 1, 2 * EDGE, side), bf16),
                pltpu.VMEM((blocks + 1, mid, side), bf16),
                pltpu.VMEM((blocks + 1, mid, side), bf16),
                pltpu.VMEM((blocks + 1, 2 * EDGE, side), bf16),
                pltpu.VMEM((blocks, 2 * side, 2 * side), jnp.float32),
                pltpu.VMEM((4 * side, 2 * side), bf16),
                dma((2 * down * across + 5,)),
                dma((2,)),
                dma((2,)),
                dma((3, tiles)),
                dma((3, tiles)),
                dma((3 * blocks + 6,)),
                dma((3 * blocks + 6,)),
                dma((4,)),
            ],
            compiler_params=pltpu.CompilerParams(collective_id=0, has_side_effects=True),
        )(
            image,
            weight,
            anchor,
            dft_tables(side),
            lens_filter_taps,
            block_src.transpose(0, 1, 3, 2),
            block_dst.transpose(0, 2, 3, 1),
            valid_count,
        )

    in_specs = (
        P("sec", "tile", None),
        P("sec", "tile", None),
        P("sec", "tile", None),
        P("sec", "tile", None, None),
        P("sec", None, "tile", None),
        P("sec", "tile", None),
        P("tile", None, None),
    )
    out_specs = P("sec", "tile", None, None)
    return jax.shard_map(body, mesh=mesh, in_specs=in_specs, out_specs=out_specs, check_vma=False)
```

```python
import functools
import math

import jax
import jax.numpy as jnp
import numpy as np
from jax import lax
from jax.experimental import pallas as pl
from jax.experimental.pallas import tpu as pltpu
from jax.sharding import PartitionSpec as P

MESH = pl.DeviceIdType.MESH
EDGE = 16
LANES = 128


def repeat(count, step):
    if count <= 4:
        for i in range(count):
            step(i)
    else:
        pl.loop(0, count)(step)


def dft_tables(size):
    positions = np.arange(size)
    angle = (positions[:, None] * positions[None, :] % size) * (2.0 * math.pi / size)
    cosine, sine = np.cos(angle), np.sin(angle)
    inverse_right = np.block([[cosine, sine], [-sine, cosine]])
    forward_left = np.block([[cosine, -sine], [-sine, -cosine]])
    return jnp.asarray(np.concatenate([inverse_right, forward_left], 0), jnp.bfloat16)


def lens(rows, taps, first, count):
    left, middle, right = rows
    lane = lax.broadcasted_iota(jnp.int32, middle.shape, 1)
    shifted = []
    for off in range(-2, 3):
        if off == 0:
            shifted.append(middle)
        elif off > 0:
            mixed = jnp.where(lane < off, right, middle)
            shifted.append(pltpu.roll(mixed, LANES - off, 1))
        else:
            mixed = jnp.where(lane >= LANES + off, left, middle)
            shifted.append(pltpu.roll(mixed, -off, 1))
    total = None
    n = middle.shape[0]
    for a in range(5):
        part = taps[5 * a] * shifted[0]
        for b in range(1, 5):
            part = part + taps[5 * a + b] * shifted[b]
        if a != 2:
            part = pltpu.roll(part, (2 - a) % n, 0)
        part = part[first : first + count]
        total = part if total is None else total + part
    return total


def kernel(
    sections,
    tiles,
    image,
    weight,
    anchor,
    tables,
    taps_any,
    src_any,
    dst_any,
    valid_any,
    out,
    taps_ref,
    src_ref,
    dst_ref,
    valid_ref,
    img,
    wgt,
    halo,
    out_mid,
    out_edge,
    in_mid,
    in_edge,
    strip_mid,
    strip_edge,
    pre_mid,
    pre_edge,
    spec,
    tab,
    load_sem,
    halo_send,
    halo_recv,
    mid_send,
    mid_recv,
    edge_send,
    edge_recv,
    strip_send,
    strip_recv,
    anchor_send,
):
    sec = lax.axis_index("sec")
    me = lax.axis_index("tile")
    th, tw = image.shape[1:]
    side = wgt.shape[1]
    blocks = strip_mid.shape[0] - 1
    cap = in_mid.shape[1]
    across, down = tw // side, th // side
    padded = across + 2
    mid = side - 2 * EDGE

    barrier = pltpu.get_barrier_semaphore()

    def greet(target):
        pl.semaphore_signal(barrier, inc=1, device_id=target, device_id_type=MESH)

    for k in range(1, tiles):
        greet((sec, lax.rem(me + k, tiles)))
    has_next, has_prev = sec < sections - 1, sec > 0
    not_first, not_last = me > 0, me < tiles - 1

    @pl.when(has_next)
    def _():
        greet((sec + 1, me))

    @pl.when(has_next & not_first)
    def _():
        greet((sec + 1, me - 1))

    @pl.when(has_prev)
    def _():
        greet((sec - 1, me))

    @pl.when(has_prev & not_last)
    def _():
        greet((sec - 1, me + 1))

    loads = []
    for source, ref in (
        (taps_any, taps_ref),
        (src_any, src_ref),
        (dst_any, dst_ref),
        (valid_any, valid_ref),
    ):
        loads.append(pltpu.make_async_copy(source, ref, load_sem.at[len(loads)]))
    for r in range(down):
        low, high = max(0, r * side - EDGE), min(th, (r + 1) * side + EDGE)
        place = low - (r * side - EDGE)
        for c in range(across):
            columns = pl.ds(c * side, side)
            loads.append(
                pltpu.make_async_copy(
                    image.at[0, pl.ds(low, high - low), columns],
                    img.at[r * padded + c + 1, pl.ds(place, high - low)],
                    load_sem.at[len(loads)],
                )
            )
            loads.append(
                pltpu.make_async_copy(
                    weight.at[0, pl.ds(r * side, side), columns],
                    wgt.at[r * across + c],
                    load_sem.at[len(loads)],
                )
            )
    table_load = pltpu.make_async_copy(tables, tab, load_sem.at[len(loads)])
    for load in loads:
        load.start()
    table_load.start()

    inner, upper, lower = pl.ds(EDGE, mid), pl.ds(0, EDGE), pl.ds(side - EDGE, EDGE)
    rim_at = 2 * blocks

    def anchor_load(j):
        for rows, ref, at in (
            (inner, pre_mid.at[j], 2 * j),
            (upper, pre_edge.at[j, pl.ds(0, EDGE)], 2 * j + 1),
            (lower, pre_edge.at[j, pl.ds(EDGE, EDGE)], 2 * j + 1),
        ):
            pltpu.make_async_copy(anchor.at[j, rows], ref, strip_recv.at[at]).start()

    @pl.when(sec == 0)
    def _():
        repeat(blocks, anchor_load)

    zeros = jnp.zeros(img.shape[1:], img.dtype)
    for r in range(down):
        img[r * padded] = zeros
        img[(r + 1) * padded - 1] = zeros

    @pl.when(me == 0)
    def _():
        for c in range(across):
            img[c + 1, :EDGE] = zeros[:EDGE]

    @pl.when(me == tiles - 1)
    def _():
        for c in range(across):
            img[(down - 1) * padded + c + 1, EDGE + side :] = zeros[:EDGE]
        for ref in (strip_mid, strip_edge, pre_mid, pre_edge):
            ref[blocks] = jnp.zeros(ref.shape[1:], ref.dtype)

    def remote(src, dst, send, recv, target):
        return pltpu.make_async_remote_copy(
            src_ref=src,
            dst_ref=dst,
            send_sem=send,
            recv_sem=recv,
            device_id=target,
            device_id_type=MESH,
        )

    halo_down = remote(
        image.at[0, pl.ds(th - EDGE, EDGE)],
        halo.at[0],
        halo_send.at[0],
        halo_recv.at[0],
        (sec, lax.rem(me + 1, tiles)),
    )
    halo_up = remote(
        image.at[0, pl.ds(0, EDGE)],
        halo.at[1],
        halo_send.at[1],
        halo_recv.at[1],
        (sec, lax.rem(me + tiles - 1, tiles)),
    )
    before_me = lax.rem(me + tiles - 1, tiles)
    next_sec = lax.rem(sec + 1, sections)
    anchor_rims = [
        remote(anchor.at[0, rows], ref, anchor_send.at[n], strip_recv.at[at], (sec, before_me))
        for n, (rows, ref, at) in enumerate(
            (
                (inner, pre_mid.at[blocks], rim_at),
                (upper, pre_edge.at[blocks, pl.ds(0, EDGE)], rim_at + 1),
                (lower, pre_edge.at[blocks, pl.ds(EDGE, EDGE)], rim_at + 1),
            )
        )
    ]
    parts = ((strip_mid, pre_mid), (strip_edge, pre_edge))

    def onward(part, j):
        strip, pre = parts[part]
        at = 2 * j + part
        return remote(strip.at[j], pre.at[j], strip_send.at[at], strip_recv.at[at], (next_sec, me))

    def onward_rim(part):
        strip, pre = parts[part]
        at = rim_at + part
        return remote(
            strip.at[0], pre.at[blocks], strip_send.at[at], strip_recv.at[at], (next_sec, before_me)
        )

    def own_rim(part):
        strip, _ = parts[part]
        at = rim_at + 2 + part
        return remote(
            strip.at[0], strip.at[blocks], strip_send.at[at], strip_recv.at[at], (sec, before_me)
        )

    def start_rims(part):
        @pl.when(has_next & not_first)
        def _():
            onward_rim(part).start()

        @pl.when(not_first)
        def _():
            own_rim(part).start()

    ahead = 1

    for load in loads:
        load.wait()

    taps = [taps_ref[0, 0, k] for k in range(25)]
    chips = tiles // 2

    def owner(k):
        chip = lax.rem(me // 2 + 1 + k // 2, chips)
        return chip * 2 + lax.rem(me + 1 + k, 2)

    def picked(target, slot, first, count):
        source = src_ref[0, 0, slot, target]
        place = source + 2 * lax.div(source, across)
        rows = [
            img[place + k, first : first + count + 2 * EDGE].astype(jnp.float32) for k in range(3)
        ]
        rows = [part[EDGE - 8 : EDGE + count + 8] for part in rows]
        corrected = lens(rows, taps, 8, count)
        factor = wgt[source, first : first + count].astype(jnp.float32)
        live = jnp.clip(valid_ref[0, 0, target] - slot, 0, 1).astype(jnp.float32)
        return (corrected * factor * live).astype(jnp.bfloat16)

    def mid_copy(k):
        target = owner(k)
        return remote(
            out_mid.at[target], in_mid.at[me], mid_send.at[target], mid_recv.at[me], (sec, target)
        )

    def edge_copy(k):
        target = owner(k)
        return remote(
            out_edge.at[target],
            in_edge.at[me],
            edge_send.at[target],
            edge_recv.at[me],
            (sec, target),
        )

    def fill_mid(k, ref, place):
        for slot in range(cap):
            for piece in range(0, mid, 32):
                ref[place, slot, piece : piece + 32] = picked(owner(k), slot, EDGE + piece, 32)

    def fill_edge(k, ref, place):
        for slot in range(cap):
            ref[place, slot, :EDGE] = picked(owner(k), slot, 0, EDGE)
            ref[place, slot, EDGE:] = picked(owner(k), slot, side - EDGE, EDGE)

    def send_mid(k):
        fill_mid(k, out_mid, owner(k))
        mid_copy(k).start()

    fill_mid(0, out_mid, owner(0))
    after, before = has_next.astype(jnp.int32), has_prev.astype(jnp.int32)
    peers = after * (1 + not_first.astype(jnp.int32)) + before * (1 + not_last.astype(jnp.int32))
    pl.semaphore_wait(barrier, tiles - 1 + peers)

    @pl.when(not_last)
    def _():
        halo_down.start()

    @pl.when(not_first)
    def _():
        halo_up.start()

    @pl.when((sec == 0) & not_first)
    def _():
        for copy in anchor_rims:
            copy.start()

    mid_copy(0).start()
    pl.loop(1, tiles - 1)(send_mid)
    fill_mid(tiles - 1, in_mid, me)

    @pl.when(not_first)
    def _():
        halo_down.wait_recv()
        for c in range(across):
            img[c + 1, :EDGE] = halo[0, :, c * side : (c + 1) * side]

    @pl.when(not_last)
    def _():
        halo_up.wait_recv()
        for c in range(across):
            img[(down - 1) * padded + c + 1, EDGE + side :] = halo[
                1, :, c * side : (c + 1) * side
            ]

    def send_edge(k):
        fill_edge(k, out_edge, owner(k))
        edge_copy(k).start()

    pl.loop(0, tiles - 1)(send_edge)
    fill_edge(tiles - 1, in_edge, me)

    def summed(ref, start, count):
        totals = [None] * blocks
        for t in range(tiles):
            for slot in range(cap):
                value = ref[t, slot, pl.ds(start, count)].astype(jnp.float32)
                place = dst_ref[0, 0, slot, t]
                for j in range(blocks):
                    term = value * (1 - jnp.minimum(jnp.abs(place - j), 1)).astype(jnp.float32)
                    totals[j] = term if totals[j] is None else totals[j] + term
        return [total.astype(jnp.bfloat16) for total in totals]

    def arrive(copy_of):
        def step(k):
            source = owner(k)
            copy_of(k, source).wait_recv()

        return step

    def mid_from(k, source):
        return remote(
            out_mid.at[source], in_mid.at[source], mid_send.at[source], mid_recv.at[source], (sec, source)
        )

    def edge_from(k, source):
        return remote(
            out_edge.at[source], in_edge.at[source], edge_send.at[source], edge_recv.at[source], (sec, source)
        )

    repeat(tiles - 1, arrive(mid_from))
    for piece in range(0, mid, 32):
        for j, value in enumerate(summed(in_mid, piece, 32)):
            strip_mid[j, piece : piece + 32] = value
    start_rims(0)

    @pl.when(has_next)
    def _():
        for j in range(ahead):
            onward(0, blocks - 1 - j).start()

    repeat(tiles - 1, arrive(edge_from))
    for j, value in enumerate(summed(in_edge, 0, 2 * EDGE)):
        strip_edge[j] = value
    start_rims(1)

    @pl.when(has_next)
    def _():
        for j in range(ahead):
            onward(1, blocks - 1 - j).start()

        def later(k):
            j = blocks - 1 - ahead - k
            onward(0, j).start()
            onward(1, j).start()

        repeat(blocks - ahead, later)


    table_load.wait()
    right_table = tab.at[pl.ds(0, 2 * side)]
    left_table = tab.at[pl.ds(2 * side, 2 * side)]

    def whole(mid_ref, edge_ref, m):
        edge = edge_ref[m]
        return jnp.concatenate([edge[:EDGE], mid_ref[m], edge[EDGE:]], 0)

    def spectra(mid_ref, edge_ref, m):
        block, after = whole(mid_ref, edge_ref, m), whole(mid_ref, edge_ref, m + 1)
        lane = lax.broadcasted_iota(jnp.int32, block.shape, 1)
        shifted = jnp.where(
            lane < side // 2, after.astype(jnp.float32), block.astype(jnp.float32)
        ).astype(block.dtype)
        windows = jnp.concatenate([block, shifted], 0)
        right = jnp.dot(
            windows, right_table[:side], preferred_element_type=jnp.float32
        ).astype(jnp.bfloat16)
        stacked = jnp.concatenate(
            [
                jnp.concatenate([right[:side, :side], right[:side, side:]], 0),
                jnp.concatenate([right[side:, :side], right[side:, side:]], 0),
            ],
            1,
        )
        return jnp.dot(left_table[...], stacked, preferred_element_type=jnp.float32)

    def keep(m):
        spec[m] = spectra(strip_mid, strip_edge, m)

    repeat(blocks - 1, keep)

    @pl.when(not_last)
    def _():
        own_rim(0).wait_recv()
        own_rim(1).wait_recv()

    keep(blocks - 1)

    @pl.when(not_last)
    def _():
        onward_rim(0).wait_recv()
        onward_rim(1).wait_recv()

    def correlate(k):
        m = blocks - 1 - k
        onward(0, m).wait_recv()
        onward(1, m).wait_recv()
        earlier = spectra(pre_mid, pre_edge, m)
        current = spec[m]
        cur_re, cur_im = current[:side], current[side:]
        pre_re, pre_im = earlier[:side], earlier[side:]
        cross_re = cur_re * pre_re + cur_im * pre_im
        cross_im = cur_im * pre_re - cur_re * pre_im
        magnitude = jnp.sqrt(cross_re * cross_re + cross_im * cross_im)
        whitened = []
        for half in range(2):
            cols = slice(half * side, (half + 1) * side)
            mag = magnitude[:, cols]
            mean = jnp.sum(mag) * (1.0 / (side * side))
            scale = (1.0 / side) / (mag + (0.1 * mean + 1e-06))
            whitened.append(
                jnp.concatenate([cross_re[:, cols] * scale, cross_im[:, cols] * scale], 1)
            )
        whitened = jnp.concatenate(whitened, 0).astype(jnp.bfloat16)
        rows = jnp.dot(
            whitened, right_table[...], preferred_element_type=jnp.float32
        ).astype(jnp.bfloat16)
        stacked = jnp.concatenate(
            [
                jnp.concatenate([rows[:side, :side], rows[:side, side:]], 0),
                jnp.concatenate([rows[side:, :side], rows[side:, side:]], 0),
            ],
            1,
        )
        result = jnp.dot(left_table[:side], stacked, preferred_element_type=jnp.float32)
        out[0, 2 * m] = result[:, :side]
        out[0, 2 * m + 1] = result[:, side:]

    repeat(blocks, correlate)

    @pl.when(not_last)
    def _():
        halo_down.wait_send()

    @pl.when(not_first)
    def _():
        halo_up.wait_send()
        own_rim(0).wait_send()
        own_rim(1).wait_send()

    @pl.when((sec == 0) & not_first)
    def _():
        for copy in anchor_rims:
            copy.wait_send()

    @pl.when(has_next)
    def _():
        def gone(j):
            onward(0, j).wait_send()
            onward(1, j).wait_send()

        repeat(blocks, gone)

    @pl.when(has_next & not_first)
    def _():
        onward_rim(0).wait_send()
        onward_rim(1).wait_send()

    def left_here(k):
        mid_copy(k).wait_send()
        edge_copy(k).wait_send()

    repeat(tiles - 1, left_here)


def solution(mesh):
    sections, tiles = mesh.shape["sec"], mesh.shape["tile"]

    def body(image, weight, lens_filter_taps, block_src, block_dst, valid_count, anchor):
        th, tw = image.shape[1:]
        blocks, side = anchor.shape[:2]
        cap = block_src.shape[-1]
        anywhere = pl.BlockSpec(memory_space=pl.ANY)
        bf16 = jnp.bfloat16
        dma = pltpu.SemaphoreType.DMA
        mid = side - 2 * EDGE
        across, down = tw // side, th // side
        return pl.pallas_call(
            functools.partial(kernel, sections, tiles),
            out_shape=pltpu.VMEM((1, 2 * blocks, side, side), jnp.float32),
            in_specs=[anywhere] * 8,
            out_specs=pl.BlockSpec(memory_space=pltpu.VMEM),
            scratch_shapes=[
                pltpu.SMEM(lens_filter_taps.shape, jnp.float32),
                pltpu.SMEM((1, 1, cap, tiles), jnp.int32),
                pltpu.SMEM((1, 1, cap, tiles), jnp.int32),
                pltpu.SMEM(valid_count.shape, jnp.int32),
                pltpu.VMEM((down * (across + 2), side + 2 * EDGE, side), bf16),
                pltpu.VMEM((down * across, side, side), bf16),
                pltpu.VMEM((2, EDGE, tw), bf16),
                pltpu.VMEM((tiles, cap, mid, side), bf16),
                pltpu.VMEM((tiles, cap, 2 * EDGE, side), bf16),
                pltpu.VMEM((tiles, cap, mid, side), bf16),
                pltpu.VMEM((tiles, cap, 2 * EDGE, side), bf16),
                pltpu.VMEM((blocks + 1, mid, side), bf16),
                pltpu.VMEM((blocks + 1, 2 * EDGE, side), bf16),
                pltpu.VMEM((blocks + 1, mid, side), bf16),
                pltpu.VMEM((blocks + 1, 2 * EDGE, side), bf16),
                pltpu.VMEM((blocks, 2 * side, 2 * side), jnp.float32),
                pltpu.VMEM((4 * side, 2 * side), bf16),
                dma((2 * down * across + 5,)),
                dma((2,)),
                dma((2,)),
                dma((tiles,)),
                dma((tiles,)),
                dma((tiles,)),
                dma((tiles,)),
                dma((2 * blocks + 4,)),
                dma((2 * blocks + 4,)),
                dma((3,)),
            ],
            compiler_params=pltpu.CompilerParams(collective_id=0, has_side_effects=True),
        )(
            image,
            weight,
            anchor,
            dft_tables(side),
            lens_filter_taps,
            block_src.transpose(0, 1, 3, 2),
            block_dst.transpose(0, 2, 3, 1),
            valid_count,
        )

    in_specs = (
        P("sec", "tile", None),
        P("sec", "tile", None),
        P("sec", "tile", None),
        P("sec", "tile", None, None),
        P("sec", None, "tile", None),
        P("sec", "tile", None),
        P("tile", None, None),
    )
    out_specs = P("sec", "tile", None, None)
    return jax.shard_map(body, mesh=mesh, in_specs=in_specs, out_specs=out_specs, check_vma=False)
```
